128 devices in a mesh: row: 16 (over x, z), col: 8 (over y, core).
Axes of the slice: x: 4, y: 4, z: 4, core: 2. Of those that a mesh axis runs over, the one named last changes fastest.
Arguments:
- features: float32 [136, 16384], P(None, 'row'), may hold values from -6 to 6
- factor: float32 [16384, 32768], P('row', 'col'), as said below
Outputs:
- panel: float32 [16384, 512], P(('row', 'col'))
The draws below stay inside these ranges and needn't reach their ends.
Inputs may be any that keep to these rules, and one draw needn't show every extreme that they name: `factor`: entries below 18 / sqrt(32768) in magnitude, and the first 512 rows of `reduced` are positive definite.
All inputs are finite; a program needn't handle non-finite values.
Results may differ from the reference program's by a relative error of at most 0.000067.
Values sent between devices are 32-bit elements; how exact they have to be, the bound alone decides.
A program may use at most 128 MiB of HBM per device.

```python
import math
import jax
import jax.numpy as jnp
from jax import lax

FEAT = 136
B = 512
R = 16384
F = 32768


def draw_factor(key, part):
    entry_scale = 3.0 / math.sqrt(F)
    entries = jnp.clip(jax.random.normal(key, (R, F), jnp.float32), -6.0, 6.0)
    return entries * entry_scale


def steps_of(rng, extent, shards, least, top_value):
    def one(dim, parts):
        draws = jax.random.uniform(jax.random.fold_in(jax.random.fold_in(rng, 6), dim), (parts,), jnp.float32, least / len(shards), top_value / len(shards))
        return jnp.repeat(jnp.exp(draws), extent[dim] // parts).reshape((-1,) + (1,) * (len(extent) - dim - 1))

    level = one(*shards[0])
    for cut in shards[1:]:
        level = level * one(*cut)
    return level


def scatter_about(key, extent, width, limit, pieces=(), kind=jnp.bfloat16):
    values = jax.random.normal(key, extent, jnp.float32) * width
    if len(pieces) > 0:
        values = steps_of(key, extent, pieces, -0.22, 0.18) * values
    return jnp.clip(values, min=-limit, max=limit).astype(kind)


def setup_inputs(seed: int = 0) -> dict:
    arg_keys = jax.random.split(jax.random.key(seed), 3)
    return {
        "features": scatter_about(arg_keys[0], (FEAT, R), 1.0, 6.0, ((1, 16),), jnp.float32),
        "factor": draw_factor(jax.random.fold_in(arg_keys[2], 71), 0),
    }


ridge_value = 40.0

def kernel(points, anchors):
    feature_count = points.shape[0]
    products = lax.dot_general(points.astype(jnp.float32), anchors.astype(jnp.float32), (((0,), (0,)), ((), ())), precision=lax.Precision.HIGHEST, preferred_element_type=jnp.float32)
    norm_points = jnp.sum(points * points, axis=0)
    norm_anchors = jnp.sum(anchors * anchors, axis=0)
    distance = norm_points[:, None] + norm_anchors[None, :] - 2.0 * products
    return products / feature_count + jnp.exp(-distance / (2.0 * feature_count))

def reference(features, factor):
    kernel_panel = kernel(features, features[:, :B])
    update = lax.dot_general(factor.astype(jnp.float32), factor[:B].astype(jnp.float32), (((1,), (1,)), ((), ())), precision=lax.Precision.HIGHEST, preferred_element_type=jnp.float32)
    identity = (jnp.arange(R, dtype=jnp.int32)[:, None] == jnp.arange(B, dtype=jnp.int32)[None, :]).astype(jnp.float32)
    reduced = kernel_panel + ridge_value * identity - update
    lower = jnp.linalg.cholesky(reduced[:B])
    solved = jax.scipy.linalg.solve_triangular(lower, reduced.T, lower=True)
    return solved.T
```

```python
import functools

import jax
import jax.numpy as jnp
from jax import lax
from jax.experimental import pallas as pl
from jax.experimental.pallas import tpu as pltpu
from jax.sharding import PartitionSpec as P

MESH = pl.DeviceIdType.MESH
HIGHEST = lax.Precision.HIGHEST
F32, BF16 = jnp.float32, jnp.bfloat16

B = 512
FEAT = 136
RIDGE = 40.0
TILE = 128
STRIP = 16
ROWS = 1024
SLAB = 512
SLABS = 8
PIECES = 32
SUB = 32
SKEW = 3
DEPTH = 5
ITEMS = 1 + PIECES + 4
SLOTS = ITEMS + SKEW * DEPTH

TREES = (
    (1, 48, 64, 48, 27, 39, 53, 36, 41, 49, 65, 49, 48, 64, 80, 64),
    (2, 23, 35, 48, 48, 40, 50, 64, 64, 58, 66, 80, 48, 46, 50, 64),
    (4, 48, 64, 48, 48, 64, 80, 64, 38, 52, 68, 52, 30, 33, 53, 45),
    (8, 48, 44, 29, 48, 64, 56, 43, 64, 80, 72, 58, 48, 64, 56, 34),
)
BLOCKS = [(i, j) for j in range(4) for i in range(j, 4)]
PLACE = {b: n for n, b in enumerate(BLOCKS)}
COLUMN = [PLACE[j, j] * TILE for j in range(4)]
SHARE = len(BLOCKS) * TILE // 8


def pick(index, table):
    value = jnp.int32(0)
    for n, entry in enumerate(table):
        value = value + jnp.where(index == n, jnp.int32(entry), jnp.int32(0))
    return value


def nt(a, b, precision=None):
    return lax.dot_general(
        a, b, (((1,), (1,)), ((), ())), precision=precision, preferred_element_type=F32
    )


def tn(a, b, precision=None):
    return lax.dot_general(
        a, b, (((0,), (0,)), ((), ())), precision=precision, preferred_element_type=F32
    )


def two_parts(x):
    high = x.astype(BF16)
    return high, (x - high.astype(F32)).astype(BF16)


def three_parts(x):
    high = x.astype(BF16)
    rest = x - high.astype(F32)
    middle = rest.astype(BF16)
    return high, middle, (rest - middle.astype(F32)).astype(BF16)


def covariance(points, anchors):
    products = tn(points, anchors, HIGHEST)
    norm_points = tn(points * points, jnp.ones((FEAT, TILE), F32), HIGHEST)[:, :1]
    norm_anchors = jnp.sum(anchors * anchors, axis=0, keepdims=True)
    distance = norm_points + norm_anchors - 2.0 * products
    return products * (1.0 / FEAT) + jnp.exp(distance * (-0.5 / FEAT))


def invert_factor(t_ref):
    ri = lax.broadcasted_iota(jnp.int32, (STRIP, TILE), 0)
    ci = lax.broadcasted_iota(jnp.int32, (STRIP, TILE), 1)
    rj = lax.broadcasted_iota(jnp.int32, (TILE, TILE), 0)
    cj = lax.broadcasted_iota(jnp.int32, (TILE, TILE), 1)

    def strip(k, carry):
        first = pl.multiple_of(k * STRIP, STRIP)
        rows = t_ref[pl.ds(first, STRIP), :]
        turned = pltpu.roll(rows, TILE - first, 1)
        cols = [jnp.broadcast_to(turned[:, c : c + 1], (STRIP, TILE)) for c in range(STRIP)]
        rows = jnp.where((ci >= first) & (ci < first + STRIP), (ci - first == ri).astype(F32), rows)
        pivots = jnp.ones((STRIP, TILE), F32)
        for c in range(STRIP):
            pivot = jnp.broadcast_to(cols[c][c : c + 1, :], (STRIP, TILE))
            pivots = jnp.where(ri == c, pivot, pivots)
            factor = jnp.where(ri > c, cols[c] * (1.0 / pivot), 0.0)
            for d in range(c + 1, STRIP):
                cols[d] = cols[d] - factor * cols[d][c : c + 1, :]
            rows = rows - factor * rows[c : c + 1, :]
        scale = lax.rsqrt(pivots)
        scale = scale * (1.5 - 0.5 * pivots * scale * scale)
        rows = rows * scale
        lh, lm, ll = three_parts(jnp.where(ci >= first + STRIP, rows, 0.0))
        rh, rm, rl = three_parts(rows)
        change = tn(
            jnp.concatenate([lh, lh, lm, lh, lm, ll], 0),
            jnp.concatenate([rh, rm, rh, rl, rm, rh], 0),
        )
        below = (cj >= first) & (cj < first + STRIP) & (rj >= first + STRIP)
        t_ref[...] = jnp.where(below, 0.0, t_ref[...]) - change
        t_ref[pl.ds(first, STRIP), :] = jnp.where(ci < first + STRIP, rows, 0.0)
        return carry

    lax.fori_loop(0, TILE // STRIP, strip, 0)


def body(
    feat_ref, factor_ref, out_ref,
    stage, high, low, land, feat_land, sums, parts, gram, gram_parts, gram_all, lower, tile, slab_kernel,
    stage_sem, piece_send, piece_recv, feat_send, feat_recv, low_send, low_recv,
    part_send, part_recv, gram_send, gram_recv,
):
    row, col = lax.axis_index("row"), lax.axis_index("col")
    x, z = row // 4, row % 4
    near = [((x + 1) % 4) * 4 + z, x * 4 + (z + 1) % 4, ((x + 3) % 4) * 4 + z, x * 4 + (z + 3) % 4]
    codes = [pick(row, table) for table in TREES]
    depth = [code // 16 for code in codes]
    sends = [[(code // (1 << d)) % 2 for d in range(4)] for code in codes]
    peers = [(col + n) % 8 for n in range(1, 8)]

    barrier = pltpu.get_barrier_semaphore()
    for d in range(4):
        pl.semaphore_signal(barrier, inc=1, device_id=(near[d], col), device_id_type=MESH)
    for peer in peers:
        pl.semaphore_signal(barrier, inc=1, device_id=(row, peer), device_id_type=MESH)
    pl.semaphore_wait(barrier, 11)

    def remote(src, dst, send, recv, device):
        return pltpu.make_async_remote_copy(
            src_ref=src, dst_ref=dst, send_sem=send, recv_sem=recv, device_id=device, device_id_type=MESH
        )

    def arrived(ref, sem):
        pltpu.make_async_copy(ref, ref, sem).wait()

    def piece_at(n, t):
        return land.at[n, pl.ds(t * SUB, SUB), :]

    def low_at(j, t):
        size = SUB * (4 - j)
        return lower.at[pl.ds(COLUMN[j] + t * size, size), :]

    def send_piece(src, n, t, d):
        remote(src, piece_at(n, t), piece_send.at[t, d], piece_recv.at[n, t], (near[d], col)).start()

    def send_features(src, t, d):
        remote(src, feat_land.at[t], feat_send.at[t, d], feat_recv.at[t], (near[d], col)).start()

    def send_low(j, t, d):
        remote(low_at(j, t), low_at(j, t), low_send.at[t, d], low_recv.at[j, t], (near[d], col)).start()

    def accumulate(slab, block, first, panel):
        panel_high, panel_low = panel
        both = jnp.concatenate([panel_high, panel_low], 0)
        a = nt(high[slab, pl.ds(first, 256), :], both)
        b = nt(low[slab, pl.ds(first, 256), :], panel_high)
        sums[block, pl.ds(first, 256), :] += a[:, :TILE] + a[:, TILE:] + b

    def send_parts(block):
        for peer in peers:
            src = sums.at[block, pl.ds(pl.multiple_of(peer * TILE, TILE), TILE), :]
            remote(src, parts.at[col, block], part_send, part_recv.at[col, block], (row, peer)).start()

    def own_points():
        return feat_ref[:, pl.ds(pl.multiple_of(col * TILE, TILE), TILE)]

    sums[...] = jnp.zeros_like(sums)

    @pl.when(row == 0)
    def root():
        for t in range(4):
            send_features(feat_ref.at[pl.ds(32 * t, 40), pl.ds(0, B)], t, t)

        def start_pieces(n, carry):
            block, slab = n // SLABS, n % SLABS
            for t in range(4):
                src = factor_ref.at[
                    pl.ds(pl.multiple_of(block * TILE + t * SUB, SUB), SUB),
                    pl.ds(pl.multiple_of(slab * SLAB, SLAB), SLAB),
                ]
                send_piece(src, n, t, t)
            return carry

        lax.fori_loop(0, PIECES, start_pieces, 0)

        def load(half, slab):
            return pltpu.make_async_copy(
                factor_ref.at[pl.ds(half * 512, 512), pl.ds(pl.multiple_of(slab * SLAB, SLAB), SLAB)],
                stage.at[slab % 2, pl.ds(half * 512, 512), :],
                stage_sem.at[half, slab % 2],
            )

        def product(half):
            load(half, 0).start()
            load(half, 1).start()

            def one(slab, carry):
                load(half, slab).wait()
                h, l = two_parts(stage[slab % 2, pl.ds(half * 512, 512), :])
                high[slab, pl.ds(half * 512, 512), :] = h
                low[slab, pl.ds(half * 512, 512), :] = l

                @pl.when(slab + 2 < SLABS)
                def _():
                    load(half, slab + 2).start()

                def block_rows(q, carry):
                    block, tile_rows = q // 2, q % 2
                    at = pl.ds(pl.multiple_of(block * TILE, TILE), TILE)
                    first = pl.multiple_of(half * 512 + tile_rows * 256, 256)
                    accumulate(slab, block, first, (high[slab, at, :], low[slab, at, :]))
                    return carry

                return lax.fori_loop(0, 8, block_rows, carry)

            lax.fori_loop(0, SLABS, one, 0)

        product(0)
        for n, (i, j) in enumerate(BLOCKS):
            gram[pl.ds(n * TILE, TILE), :] = sums[j, pl.ds(i * TILE, TILE), :]
        mine = pl.ds(pl.multiple_of(col * SHARE, SHARE), SHARE)
        for peer in peers:
            src = gram.at[pl.ds(pl.multiple_of(peer * SHARE, SHARE), SHARE), :]
            remote(src, gram_parts.at[col], gram_send.at[0], gram_recv.at[0, col], (row, peer)).start()
        product(1)
        share = gram[mine, :]
        for peer in peers:
            arrived(gram_parts.at[peer], gram_recv.at[0, peer])
            share = share + gram_parts[peer]
        gram_all[mine, :] = share
        for peer in peers:
            remote(
                gram_all.at[mine, :], gram_all.at[mine, :], gram_send.at[1], gram_recv.at[1, col], (row, peer)
            ).start()
        for j in range(4):
            size = (4 - j) * TILE
            values = covariance(feat_ref[:, j * TILE : B], feat_ref[:, j * TILE : (j + 1) * TILE])
            same = lax.broadcasted_iota(jnp.int32, (size, TILE), 0) == lax.broadcasted_iota(jnp.int32, (size, TILE), 1)
            lower[pl.ds(COLUMN[j], size), :] = values + jnp.where(same, RIDGE, 0.0)
        slab_kernel[...] = covariance(own_points(), feat_ref[:, :B])
        for peer in peers:
            arrived(gram_all.at[pl.ds(pl.multiple_of(peer * SHARE, SHARE), SHARE), :], gram_recv.at[1, peer])
        lower[...] = lower[...] - gram_all[...]
        for block in range(4):
            send_parts(block)

        def at(i, j):
            return pl.ds(PLACE[i, j] * TILE, TILE)

        for j in range(4):
            tile[...] = lower[at(j, j), :]
            invert_factor(tile)
            inverse = tile[...]
            lower[at(j, j), :] = inverse
            for i in range(j + 1, 4):
                lower[at(i, j), :] = nt(lower[at(i, j), :], inverse, HIGHEST)
            for t in range(4):
                send_low(j, t, t)
            for k in range(j + 1, 4):
                for i in range(k, 4):
                    lower[at(i, k), :] = lower[at(i, k), :] - nt(lower[at(i, j), :], lower[at(k, j), :], HIGHEST)

    @pl.when(row != 0)
    def others():
        def load(slab):
            return pltpu.make_async_copy(
                factor_ref.at[:, pl.ds(pl.multiple_of(slab * SLAB, SLAB), SLAB)],
                stage.at[slab % 2],
                stage_sem.at[0, slab % 2],
            )

        load(0).start()
        load(1).start()

        def slot(s, carry):
            for t in range(4):
                item = s - SKEW * depth[t]

                @pl.when(item == 0)
                def _():
                    arrived(feat_land.at[t], feat_recv.at[t])
                    for d in range(4):
                        @pl.when(sends[t][d] == 1)
                        def _():
                            send_features(feat_land.at[t], t, d)

                @pl.when((item >= 1) & (item <= PIECES))
                def _():
                    n = item - 1
                    arrived(piece_at(n, t), piece_recv.at[n, t])
                    for d in range(4):
                        @pl.when(sends[t][d] == 1)
                        def _():
                            send_piece(piece_at(n, t), n, t, d)

                for j in range(4):
                    @pl.when(item == PIECES + 1 + j)
                    def _():
                        arrived(low_at(j, t), low_recv.at[j, t])
                        for d in range(4):
                            @pl.when(sends[t][d] == 1)
                            def _():
                                send_low(j, t, d)

            @pl.when(s < SLABS)
            def _():
                load(s).wait()
                h, l = two_parts(stage[s % 2])
                high[s] = h
                low[s] = l

                @pl.when(s + 2 < SLABS)
                def _():
                    load(s + 2).start()

            @pl.when(s == SKEW * DEPTH)
            def _():
                anchors = jnp.concatenate([feat_land[t, :32] for t in range(3)] + [feat_land[3]], 0)
                slab_kernel[...] = covariance(own_points(), anchors)

            m = s - SKEW * DEPTH - 1

            @pl.when((m >= 0) & (m < PIECES))
            def _():
                block, slab = m // SLABS, m % SLABS
                panel = two_parts(land[m])

                def tile_rows(q, carry):
                    accumulate(slab, block, pl.multiple_of(q * 256, 256), panel)
                    return carry

                lax.fori_loop(0, ROWS // 256, tile_rows, 0)

                @pl.when(slab == SLABS - 1)
                def _():
                    send_parts(block)

            return carry

        lax.fori_loop(0, SLOTS, slot, 0)

    solved = []
    rows = lax.broadcasted_iota(jnp.int32, (TILE, TILE), 0) + row * ROWS + col * TILE
    columns = lax.broadcasted_iota(jnp.int32, (TILE, TILE), 1)
    for j in range(4):
        value = slab_kernel[:, j * TILE : (j + 1) * TILE]
        value = value + jnp.where(rows == columns + j * TILE, RIDGE, 0.0)
        total = sums[j, pl.ds(pl.multiple_of(col * TILE, TILE), TILE), :]
        for peer in peers:
            arrived(parts.at[peer, j], part_recv.at[peer, j])
            total = total + parts[peer, j]
        value = value - total
        for i in range(j):
            value = value - nt(solved[i], lower[pl.ds(PLACE[j, i] * TILE, TILE), :], HIGHEST)
        solved.append(nt(value, lower[pl.ds(PLACE[j, j] * TILE, TILE), :], HIGHEST))
        out_ref[:, j * TILE : (j + 1) * TILE] = solved[j]

    arrived(sums.at[:, pl.ds(0, 7 * TILE), :], part_send)
    for t in range(4):
        for d in range(4):
            @pl.when(sends[t][d] == 1)
            def _():
                arrived(land.at[:, pl.ds(0, SUB), :], piece_send.at[t, d])
                arrived(feat_land.at[t], feat_send.at[t, d])
                arrived(lower.at[pl.ds(0, 10 * SUB), :], low_send.at[t, d])

    @pl.when(row == 0)
    def _():
        for phase in range(2):
            arrived(gram_parts.at[pl.ds(0, 7)], gram_send.at[phase])


def on_device(features, factor):
    dma = pltpu.SemaphoreType.DMA
    return pl.pallas_call(
        body,
        out_shape=jax.ShapeDtypeStruct((TILE, B), F32),
        in_specs=[pl.BlockSpec(memory_space=pltpu.VMEM), pl.BlockSpec(memory_space=pl.ANY)],
        out_specs=pl.BlockSpec(memory_space=pltpu.VMEM),
        scratch_shapes=[
            pltpu.VMEM((2, ROWS, SLAB), F32),
            pltpu.VMEM((SLABS, ROWS, SLAB), BF16),
            pltpu.VMEM((SLABS, ROWS, SLAB), BF16),
            pltpu.VMEM((PIECES, TILE, SLAB), F32),
            pltpu.VMEM((4, 40, B), F32),
            pltpu.VMEM((4, ROWS, TILE), F32),
            pltpu.VMEM((8, 4, TILE, TILE), F32),
            pltpu.VMEM((10 * TILE, TILE), F32),
            pltpu.VMEM((8, SHARE, TILE), F32),
            pltpu.VMEM((10 * TILE, TILE), F32),
            pltpu.VMEM((10 * TILE, TILE), F32),
            pltpu.VMEM((TILE, TILE), F32),
            pltpu.VMEM((TILE, B), F32),
            dma((2, 2)),
            dma((4, 4)),
            dma((PIECES, 4)),
            dma((4, 4)),
            dma((4,)),
            dma((4, 4)),
            dma((4, 4)),
            dma,
            dma((8, 4)),
            dma((2,)),
            dma((2, 8)),
        ],
        compiler_params=pltpu.CompilerParams(
            collective_id=0, has_side_effects=True, vmem_limit_bytes=56 << 20
        ),
    )(features, factor)


def solution(mesh):
    placed = (P(None, "row"), P("row", "col"))
    return jax.shard_map(
        on_device, mesh=mesh, in_specs=placed, out_specs=P(("row", "col"), None), check_vma=False
    )
```

```python
import functools

import jax
import jax.numpy as jnp
from jax import lax
from jax.experimental import pallas as pl
from jax.experimental.pallas import tpu as pltpu
from jax.sharding import PartitionSpec as P

MESH = pl.DeviceIdType.MESH
HIGHEST = lax.Precision.HIGHEST
F32, BF16 = jnp.float32, jnp.bfloat16

B = 512
FEAT = 136
RIDGE = 40.0
TILE = 128
STRIP = 16
ROWS = 1024
SLAB = 512
SLABS = 8
PIECES = 32
SUB = 32
AHEAD = 8
SKEW = 3
DEPTH = 5
ITEMS = 1 + PIECES + 4
SLOTS = ITEMS + SKEW * DEPTH

TREES = (
    (1, 48, 64, 48, 27, 39, 53, 36, 41, 49, 65, 49, 48, 64, 80, 64),
    (2, 23, 35, 48, 48, 40, 50, 64, 64, 58, 66, 80, 48, 46, 50, 64),
    (4, 48, 64, 48, 48, 64, 80, 64, 38, 52, 68, 52, 30, 33, 53, 45),
    (8, 48, 44, 29, 48, 64, 56, 43, 64, 80, 72, 58, 48, 64, 56, 34),
)
BLOCKS = [(i, j) for j in range(4) for i in range(j, 4)]
PLACE = {b: n for n, b in enumerate(BLOCKS)}
COLUMN = [PLACE[j, j] * TILE for j in range(4)]
SHARE = len(BLOCKS) * TILE // 8


def pick(index, table):
    value = jnp.int32(0)
    for n, entry in enumerate(table):
        value = value + jnp.where(index == n, jnp.int32(entry), jnp.int32(0))
    return value


def nt(a, b, precision=None):
    return lax.dot_general(
        a, b, (((1,), (1,)), ((), ())), precision=precision, preferred_element_type=F32
    )


def tn(a, b, precision=None):
    return lax.dot_general(
        a, b, (((0,), (0,)), ((), ())), precision=precision, preferred_element_type=F32
    )


def two_parts(x):
    high = x.astype(BF16)
    return high, (x - high.astype(F32)).astype(BF16)


def three_parts(x):
    high = x.astype(BF16)
    rest = x - high.astype(F32)
    middle = rest.astype(BF16)
    return high, middle, (rest - middle.astype(F32)).astype(BF16)


def covariance(points, anchors):
    products = tn(points, anchors, HIGHEST)
    norm_points = tn(points * points, jnp.ones((FEAT, TILE), F32), HIGHEST)[:, :1]
    norm_anchors = jnp.sum(anchors * anchors, axis=0, keepdims=True)
    distance = norm_points + norm_anchors - 2.0 * products
    return products * (1.0 / FEAT) + jnp.exp(distance * (-0.5 / FEAT))


def invert_factor(t_ref):
    ri = lax.broadcasted_iota(jnp.int32, (STRIP, TILE), 0)
    ci = lax.broadcasted_iota(jnp.int32, (STRIP, TILE), 1)
    rj = lax.broadcasted_iota(jnp.int32, (TILE, TILE), 0)
    cj = lax.broadcasted_iota(jnp.int32, (TILE, TILE), 1)

    def strip(k, carry):
        first = pl.multiple_of(k * STRIP, STRIP)
        rows = t_ref[pl.ds(first, STRIP), :]
        turned = pltpu.roll(rows, TILE - first, 1)
        cols = [jnp.broadcast_to(turned[:, c : c + 1], (STRIP, TILE)) for c in range(STRIP)]
        rows = jnp.where((ci >= first) & (ci < first + STRIP), (ci - first == ri).astype(F32), rows)
        pivots = jnp.ones((STRIP, TILE), F32)
        for c in range(STRIP):
            pivot = jnp.broadcast_to(cols[c][c : c + 1, :], (STRIP, TILE))
            pivots = jnp.where(ri == c, pivot, pivots)
            factor = jnp.where(ri > c, cols[c] * (1.0 / pivot), 0.0)
            for d in range(c + 1, STRIP):
                cols[d] = cols[d] - factor * cols[d][c : c + 1, :]
            rows = rows - factor * rows[c : c + 1, :]
        scale = lax.rsqrt(pivots)
        scale = scale * (1.5 - 0.5 * pivots * scale * scale)
        rows = rows * scale
        lh, lm, ll = three_parts(jnp.where(ci >= first + STRIP, rows, 0.0))
        rh, rm, rl = three_parts(rows)
        change = tn(
            jnp.concatenate([lh, lh, lm, lh, lm, ll], 0),
            jnp.concatenate([rh, rm, rh, rl, rm, rh], 0),
        )
        below = (cj >= first) & (cj < first + STRIP) & (rj >= first + STRIP)
        t_ref[...] = jnp.where(below, 0.0, t_ref[...]) - change
        t_ref[pl.ds(first, STRIP), :] = jnp.where(ci < first + STRIP, rows, 0.0)
        return carry

    lax.fori_loop(0, TILE // STRIP, strip, 0)


def body(
    feat_ref, factor_ref, out_ref,
    stage, high, low, land, feat_land, sums, pair, parts, own, gram, gram_parts, gram_all, lower, tile, slab_kernel,
    stage_sem, piece_send, piece_recv, feat_send, feat_recv, low_send, low_recv,
    pair_send, pair_recv, part_send, part_recv, gram_send, gram_recv,
):
    row, col = lax.axis_index("row"), lax.axis_index("col")
    x, z = row // 4, row % 4
    near = [((x + 1) % 4) * 4 + z, x * 4 + (z + 1) % 4, ((x + 3) % 4) * 4 + z, x * 4 + (z + 3) % 4]
    codes = [pick(row, table) for table in TREES]
    depth = [code // 16 for code in codes]
    sends = [[(code // (1 << d)) % 2 for d in range(4)] for code in codes]
    peers = [(col + n) % 8 for n in range(1, 8)]
    y, core = col // 2, col % 2
    sibling = y * 2 + 1 - core
    pivot = (row == 0) & (col < 4)

    barrier = pltpu.get_barrier_semaphore()
    for d in range(4):
        pl.semaphore_signal(barrier, inc=1, device_id=(near[d], col), device_id_type=MESH)
    for peer in peers:
        pl.semaphore_signal(barrier, inc=1, device_id=(row, peer), device_id_type=MESH)
    pl.semaphore_wait(barrier, 11)

    def remote(src, dst, send, recv, device):
        return pltpu.make_async_remote_copy(
            src_ref=src, dst_ref=dst, send_sem=send, recv_sem=recv, device_id=device, device_id_type=MESH
        )

    def arrived(ref, sem):
        pltpu.make_async_copy(ref, ref, sem).wait()

    def piece_at(n, t):
        return land.at[n, pl.ds(t * SUB, SUB), :]

    def low_at(j, t):
        size = SUB * (4 - j)
        return lower.at[pl.ds(COLUMN[j] + t * size, size), :]

    def send_piece(src, n, t, d):
        remote(src, piece_at(n, t), piece_send.at[t, d], piece_recv.at[n, t], (near[d], col)).start()

    def send_features(src, t, d):
        remote(src, feat_land.at[t], feat_send.at[t, d], feat_recv.at[t], (near[d], col)).start()

    def send_low(j, t, d):
        remote(low_at(j, t), low_at(j, t), low_send.at[t, d], low_recv.at[j, t], (near[d], col)).start()

    def accumulate(slab, block, panel):
        panel_high, panel_low = panel
        a = nt(high[slab], jnp.concatenate([panel_high, panel_low], 0))
        b = nt(low[slab], panel_high)
        sums[block] += a[:, :TILE] + a[:, TILE:] + b

    def owned(q, c):
        return pl.ds(pl.multiple_of((q * 2 + c) * TILE, TILE), TILE)

    def send_pair(block, first):
        for q in range(first, 4):
            src = sums.at[block, owned(q, 1 - core), :]
            remote(src, pair.at[block, q], pair_send, pair_recv.at[block], (row, sibling)).start()

    def send_parts(block, first):
        arrived(pair.at[block, pl.ds(first, 4 - first)], pair_recv.at[block])
        for q in range(first, 4):
            sums[block, owned(q, core), :] += pair[block, q]

            @pl.when(q != y)
            def _():
                src = sums.at[block, owned(q, core), :]
                remote(src, parts.at[block, y], part_send, part_recv.at[block, y], (row, q * 2 + core)).start()

    def own_points():
        return feat_ref[:, pl.ds(pl.multiple_of(col * TILE, TILE), TILE)]

    sums[...] = jnp.zeros_like(sums)

    @pl.when(row == 0)
    def root():
        for t in range(4):
            send_features(feat_ref.at[pl.ds(32 * t, 40), pl.ds(0, B)], t, t)

        def start_piece(n, carry):
            block, slab = n // SLABS, n % SLABS
            for t in range(4):
                src = factor_ref.at[
                    pl.ds(pl.multiple_of(block * TILE + t * SUB, SUB), SUB),
                    pl.ds(pl.multiple_of(slab * SLAB, SLAB), SLAB),
                ]
                send_piece(src, n, t, t)
            return carry

        lax.fori_loop(0, AHEAD, start_piece, 0)

        def load(half, slab):
            return pltpu.make_async_copy(
                factor_ref.at[pl.ds(half * 512, 512), pl.ds(pl.multiple_of(slab * SLAB, SLAB), SLAB)],
                stage.at[slab % 2, pl.ds(half * 512, 512), :],
                stage_sem.at[half, slab % 2],
            )

        def product(half, begin, end):
            def one(slab, carry):
                if half == 0:
                    carry = lax.fori_loop(AHEAD + slab * 3, AHEAD + slab * 3 + 3, start_piece, carry)
                load(half, slab).wait()
                h, l = two_parts(stage[slab % 2, pl.ds(half * 512, 512), :])
                high[slab, pl.ds(half * 512, 512), :] = h
                low[slab, pl.ds(half * 512, 512), :] = l

                @pl.when(slab + 2 < SLABS)
                def _():
                    load(half, slab + 2).start()

                panel_high, panel_low = high[slab, :512], low[slab, :512]
                if half == 0:
                    total = nt(h, panel_high * 0.5) + nt(h, panel_low)
                else:
                    total = nt(h, panel_high) + nt(h, panel_low) + nt(l, panel_high)
                for block in range(4):
                    sums[block, pl.ds(half * 512, 512), :] += total[:, block * TILE : (block + 1) * TILE]
                return carry

            lax.fori_loop(begin, end, one, 0)

        for half in range(2):
            load(half, 0).start()
            load(half, 1).start()
        product(0, 0, SLABS)
        for n, (i, j) in enumerate(BLOCKS):
            gram[pl.ds(n * TILE, TILE), :] = sums[j, pl.ds(i * TILE, TILE), :] + sums[i, pl.ds(j * TILE, TILE), :].T
        mine = pl.ds(pl.multiple_of(col * SHARE, SHARE), SHARE)
        for peer in peers:
            src = gram.at[pl.ds(pl.multiple_of(peer * SHARE, SHARE), SHARE), :]
            remote(src, gram_parts.at[col], gram_send.at[0], gram_recv.at[0, col], (row, peer)).start()
        product(1, 0, 4)
        share = gram[mine, :]
        for peer in peers:
            arrived(gram_parts.at[peer], gram_recv.at[0, peer])
            share = share + gram_parts[peer]
        gram_all[mine, :] = share
        for peer in peers:
            remote(
                gram_all.at[mine, :], gram_all.at[mine, :], gram_send.at[1], gram_recv.at[1, col], (row, peer)
            ).start()
        for j in range(4):
            size = (4 - j) * TILE
            values = covariance(feat_ref[:, j * TILE : B], feat_ref[:, j * TILE : (j + 1) * TILE])
            same = lax.broadcasted_iota(jnp.int32, (size, TILE), 0) == lax.broadcasted_iota(jnp.int32, (size, TILE), 1)
            lower[pl.ds(COLUMN[j], size), :] = values + jnp.where(same, RIDGE, 0.0)
        for peer in peers:
            arrived(gram_all.at[pl.ds(pl.multiple_of(peer * SHARE, SHARE), SHARE), :], gram_recv.at[1, peer])
        lower[...] = lower[...] - gram_all[...]

        def at(i, j):
            return pl.ds(PLACE[i, j] * TILE, TILE)

        for j in range(4):
            tile[...] = lower[at(j, j), :]
            invert_factor(tile)
            inverse = tile[...]
            lower[at(j, j), :] = inverse
            for i in range(j + 1, 4):
                lower[at(i, j), :] = nt(lower[at(i, j), :], inverse, HIGHEST)
            for t in range(4):
                send_low(j, t, t)
            for k in range(j + 1, 4):
                for i in range(k, 4):
                    lower[at(i, k), :] = lower[at(i, k), :] - nt(lower[at(i, j), :], lower[at(k, j), :], HIGHEST)
        product(1, 4, SLABS)
        for block in range(4):
            send_pair(block, 2)
        slab_kernel[...] = covariance(own_points(), feat_ref[:, :B])
        for block in range(4):
            send_parts(block, 2)

    @pl.when(row != 0)
    def others():
        def load(slab):
            return pltpu.make_async_copy(
                factor_ref.at[:, pl.ds(pl.multiple_of(slab * SLAB, SLAB), SLAB)],
                stage.at[slab % 2],
                stage_sem.at[0, slab % 2],
            )

        load(0).start()
        load(1).start()

        def slot(s, carry):
            for t in range(4):
                item = s - SKEW * depth[t]

                @pl.when(item == 0)
                def _():
                    arrived(feat_land.at[t], feat_recv.at[t])
                    for d in range(4):
                        @pl.when(sends[t][d] == 1)
                        def _():
                            send_features(feat_land.at[t], t, d)

                @pl.when((item >= 1) & (item <= PIECES))
                def _():
                    n = item - 1
                    arrived(piece_at(n, t), piece_recv.at[n, t])
                    for d in range(4):
                        @pl.when(sends[t][d] == 1)
                        def _():
                            send_piece(piece_at(n, t), n, t, d)

                for j in range(4):
                    @pl.when(item == PIECES + 1 + j)
                    def _():
                        arrived(low_at(j, t), low_recv.at[j, t])
                        for d in range(4):
                            @pl.when(sends[t][d] == 1)
                            def _():
                                send_low(j, t, d)

            @pl.when(s < SLABS)
            def _():
                load(s).wait()
                h, l = two_parts(stage[s % 2])
                high[s] = h
                low[s] = l

                @pl.when(s + 2 < SLABS)
                def _():
                    load(s + 2).start()

            @pl.when(s == SKEW * DEPTH)
            def _():
                anchors = jnp.concatenate([feat_land[t, :32] for t in range(3)] + [feat_land[3]], 0)
                slab_kernel[...] = covariance(own_points(), anchors)

            m = s - SKEW * DEPTH - 1

            @pl.when((m >= 0) & (m < PIECES))
            def _():
                block, slab = m // SLABS, m % SLABS
                accumulate(slab, block, two_parts(land[m]))

                @pl.when(slab == SLABS - 1)
                def _():
                    send_pair(block, 0)

                @pl.when((slab == 1) & (block > 0))
                def _():
                    send_parts(block - 1, 0)

            return carry

        lax.fori_loop(0, SLOTS, slot, 0)

    solved = []
    rows = lax.broadcasted_iota(jnp.int32, (TILE, TILE), 0) + row * ROWS + col * TILE
    columns = lax.broadcasted_iota(jnp.int32, (TILE, TILE), 1)

    def rest(j):
        value = slab_kernel[:, j * TILE : (j + 1) * TILE]
        value = value + jnp.where(rows == columns + j * TILE, RIDGE, 0.0)
        for i in range(j):
            value = value - nt(solved[i], lower[pl.ds(PLACE[j, i] * TILE, TILE), :], HIGHEST)
        return value

    def solve(j, value):
        @pl.when(pivot)
        def _():
            place = COLUMN[j] + jnp.maximum(col - j, 0) * TILE
            own[...] = gram_all[pl.ds(pl.multiple_of(place, TILE), TILE), :]

        @pl.when(jnp.logical_not(pivot))
        def _():
            own[...] = sums[j, owned(y, core), :]
            for n in range(1, 4):
                other = (y + n) % 4
                arrived(parts.at[j, other], part_recv.at[j, other])
                own[...] += parts[j, other]

        value = nt(value - own[...], lower[pl.ds(PLACE[j, j] * TILE, TILE), :], HIGHEST)
        value = jnp.where(pivot & (col < j), 0.0, value)
        solved.append(value)
        out_ref[:, j * TILE : (j + 1) * TILE] = value

    solve(0, rest(0))

    @pl.when(row != 0)
    def _():
        send_parts(3, 0)

    for j in range(1, 4):
        solve(j, rest(j))

    @pl.when(row != 0)
    def _():
        arrived(pair, pair_send)
        arrived(parts.at[:, pl.ds(0, 3)], part_send)

    @pl.when(row == 0)
    def _():
        arrived(pair.at[:, pl.ds(0, 2)], pair_send)

        @pl.when(pivot)
        def _():
            arrived(parts.at[:, pl.ds(0, 2)], part_send)

        @pl.when(jnp.logical_not(pivot))
        def _():
            arrived(parts.at[:, 0], part_send)

    for t in range(4):
        for d in range(4):
            @pl.when(sends[t][d] == 1)
            def _():
                arrived(land.at[:, pl.ds(0, SUB), :], piece_send.at[t, d])
                arrived(feat_land.at[t], feat_send.at[t, d])
                arrived(lower.at[pl.ds(0, 10 * SUB), :], low_send.at[t, d])

    @pl.when(row == 0)
    def _():
        for phase in range(2):
            arrived(gram_parts.at[pl.ds(0, 7)], gram_send.at[phase])


def on_device(features, factor):
    dma = pltpu.SemaphoreType.DMA
    return pl.pallas_call(
        body,
        out_shape=jax.ShapeDtypeStruct((TILE, B), F32),
        in_specs=[pl.BlockSpec(memory_space=pltpu.VMEM), pl.BlockSpec(memory_space=pl.ANY)],
        out_specs=pl.BlockSpec(memory_space=pltpu.VMEM),
        scratch_shapes=[
            pltpu.VMEM((2, ROWS, SLAB), F32),
            pltpu.VMEM((SLABS, ROWS, SLAB), BF16),
            pltpu.VMEM((SLABS, ROWS, SLAB), BF16),
            pltpu.VMEM((PIECES, TILE, SLAB), F32),
            pltpu.VMEM((4, 40, B), F32),
            pltpu.VMEM((4, ROWS, TILE), F32),
            pltpu.VMEM((4, 4, TILE, TILE), F32),
            pltpu.VMEM((4, 4, TILE, TILE), F32),
            pltpu.VMEM((TILE, TILE), F32),
            pltpu.VMEM((10 * TILE, TILE), F32),
            pltpu.VMEM((8, SHARE, TILE), F32),
            pltpu.VMEM((10 * TILE, TILE), F32),
            pltpu.VMEM((10 * TILE, TILE), F32),
            pltpu.VMEM((TILE, TILE), F32),
            pltpu.VMEM((TILE, B), F32),
            dma((2, 2)),
            dma((4, 4)),
            dma((PIECES, 4)),
            dma((4, 4)),
            dma((4,)),
            dma((4, 4)),
            dma((4, 4)),
            dma,
            dma((4,)),
            dma,
            dma((4, 4)),
            dma((2,)),
            dma((2, 8)),
        ],
        compiler_params=pltpu.CompilerParams(
            collective_id=0, has_side_effects=True, vmem_limit_bytes=56 << 20
        ),
    )(features, factor)


def solution(mesh):
    placed = (P(None, "row"), P("row", "col"))
    return jax.shard_map(
        on_device, mesh=mesh, in_specs=placed, out_specs=P(("row", "col"), None), check_vma=False
    )
```

```python
import functools

import jax
import jax.numpy as jnp
from jax import lax
from jax.experimental import pallas as pl
from jax.experimental.pallas import tpu as pltpu
from jax.sharding import PartitionSpec as P

MESH = pl.DeviceIdType.MESH
HIGHEST = lax.Precision.HIGHEST
F32, BF16 = jnp.float32, jnp.bfloat16

B = 512
FEAT = 136
RIDGE = 40.0
TILE = 128
STRIP = 16
ROWS = 1024
SLAB = 512
SLABS = 8
PIECES = 32
SUB = 32
AHEAD = 8
ITEMS = PIECES + 1 + 4

TREES = (
    (1, 48, 64, 48, 27, 39, 53, 36, 41, 49, 65, 49, 48, 64, 80, 64),
    (2, 23, 35, 48, 48, 40, 50, 64, 64, 58, 66, 80, 48, 46, 50, 64),
    (4, 48, 64, 48, 48, 64, 80, 64, 38, 52, 68, 52, 30, 33, 53, 45),
    (8, 48, 44, 29, 48, 64, 56, 43, 64, 80, 72, 58, 48, 64, 56, 34),
)
BLOCKS = [(i, j) for j in range(4) for i in range(j, 4)]
PLACE = {b: n for n, b in enumerate(BLOCKS)}
COLUMN = [PLACE[j, j] * TILE for j in range(4)]
SHARE = len(BLOCKS) * TILE // 8


def lag(depth):
    return depth * 3 - 1


def pick(index, table):
    value = jnp.int32(0)
    for n, entry in enumerate(table):
        value = value + jnp.where(index == n, jnp.int32(entry), jnp.int32(0))
    return value


def nt(a, b, precision=None):
    return lax.dot_general(
        a, b, (((1,), (1,)), ((), ())), precision=precision, preferred_element_type=F32
    )


def tn(a, b, precision=None):
    return lax.dot_general(
        a, b, (((0,), (0,)), ((), ())), precision=precision, preferred_element_type=F32
    )


def two_parts(x):
    high = x.astype(BF16)
    return high, (x - high.astype(F32)).astype(BF16)


def three_parts(x):
    high = x.astype(BF16)
    rest = x - high.astype(F32)
    middle = rest.astype(BF16)
    return high, middle, (rest - middle.astype(F32)).astype(BF16)


def covariance(points, anchors):
    products = tn(points, anchors, HIGHEST)
    norm_points = tn(points * points, jnp.ones((FEAT, TILE), F32), HIGHEST)[:, :1]
    norm_anchors = jnp.sum(anchors * anchors, axis=0, keepdims=True)
    distance = norm_points + norm_anchors - 2.0 * products
    return products * (1.0 / FEAT) + jnp.exp(distance * (-0.5 / FEAT))


def invert_factor(t_ref):
    ri = lax.broadcasted_iota(jnp.int32, (STRIP, TILE), 0)
    ci = lax.broadcasted_iota(jnp.int32, (STRIP, TILE), 1)
    rj = lax.broadcasted_iota(jnp.int32, (TILE, TILE), 0)
    cj = lax.broadcasted_iota(jnp.int32, (TILE, TILE), 1)

    def strip(k, carry):
        first = pl.multiple_of(k * STRIP, STRIP)
        rows = t_ref[pl.ds(first, STRIP), :]
        turned = pltpu.roll(rows, TILE - first, 1)
        cols = [jnp.broadcast_to(turned[:, c : c + 1], (STRIP, TILE)) for c in range(STRIP)]
        rows = jnp.where((ci >= first) & (ci < first + STRIP), (ci - first == ri).astype(F32), rows)
        pivots = jnp.ones((STRIP, TILE), F32)
        for c in range(STRIP):
            pivot = jnp.broadcast_to(cols[c][c : c + 1, :], (STRIP, TILE))
            pivots = jnp.where(ri == c, pivot, pivots)
            factor = jnp.where(ri > c, cols[c] * (1.0 / pivot), 0.0)
            for d in range(c + 1, STRIP):
                cols[d] = cols[d] - factor * cols[d][c : c + 1, :]
            rows = rows - factor * rows[c : c + 1, :]
        scale = lax.rsqrt(pivots)
        scale = scale * (1.5 - 0.5 * pivots * scale * scale)
        rows = rows * scale
        lh, lm, ll = three_parts(jnp.where(ci >= first + STRIP, rows, 0.0))
        rh, rm, rl = three_parts(rows)
        change = tn(
            jnp.concatenate([lh, lh, lm, lh, lm, ll], 0),
            jnp.concatenate([rh, rm, rh, rl, rm, rh], 0),
        )
        below = (cj >= first) & (cj < first + STRIP) & (rj >= first + STRIP)
        t_ref[...] = jnp.where(below, 0.0, t_ref[...]) - change
        t_ref[pl.ds(first, STRIP), :] = jnp.where(ci < first + STRIP, rows, 0.0)
        return carry

    lax.fori_loop(0, TILE // STRIP, strip, 0)


def body(
    feat_ref, factor_ref, out_ref,
    stage, high, low, land, feat_land, sums, pair, parts, own, gram, gram_parts, gram_all, lower, tile, slab_kernel,
    stage_sem, piece_send, piece_recv, feat_send, feat_recv, low_send, low_recv,
    pair_send, pair_recv, part_send, part_recv, gram_send, gram_recv, share_send, share_recv,
):
    row, col = lax.axis_index("row"), lax.axis_index("col")
    x, z = row // 4, row % 4
    near = [((x + 1) % 4) * 4 + z, x * 4 + (z + 1) % 4, ((x + 3) % 4) * 4 + z, x * 4 + (z + 3) % 4]
    codes = [pick(row, table) for table in TREES]
    depth = [code // 16 for code in codes]
    sends = [[(code // (1 << d)) % 2 for d in range(4)] for code in codes]
    peers = [(col + n) % 8 for n in range(1, 8)]
    y, core = col // 2, col % 2
    sibling = y * 2 + 1 - core
    pivot = (row == 0) & (col < 4)
    lags = [lag(d) for d in depth]
    last = jnp.maximum(jnp.maximum(lags[0], lags[1]), jnp.maximum(lags[2], lags[3]))

    barrier = pltpu.get_barrier_semaphore()
    for d in range(4):
        pl.semaphore_signal(barrier, inc=1, device_id=(near[d], col), device_id_type=MESH)
    for peer in peers:
        pl.semaphore_signal(barrier, inc=1, device_id=(row, peer), device_id_type=MESH)
    pl.semaphore_wait(barrier, 11)

    def remote(src, dst, send, recv, device):
        return pltpu.make_async_remote_copy(
            src_ref=src, dst_ref=dst, send_sem=send, recv_sem=recv, device_id=device, device_id_type=MESH
        )

    def arrived(ref, sem):
        pltpu.make_async_copy(ref, ref, sem).wait()

    def piece_at(n, t):
        return land.at[n, pl.ds(t * SUB, SUB), :]

    def low_at(j, t, c):
        size = SUB // 2 * (4 - j)
        return lower.at[pl.ds(pl.multiple_of(COLUMN[j] + (2 * t + c) * size, 16), size), :]

    def feat_at(t, c):
        return feat_land.at[t, :, pl.ds(pl.multiple_of(c * (B // 2), TILE), B // 2)]

    def exchange(ref, item, t):
        remote(ref, ref, share_send, share_recv.at[item, t], (row, sibling)).start()

    def send_piece(src, n, t, d):
        remote(src, piece_at(n, t), piece_send.at[t, d], piece_recv.at[n, t], (near[d], col)).start()

    def send_features(src, t, d):
        remote(src, feat_at(t, core), feat_send.at[t, d], feat_recv.at[t], (near[d], col)).start()

    def send_low(j, t, d):
        remote(low_at(j, t, core), low_at(j, t, core), low_send.at[t, d], low_recv.at[j, t], (near[d], col)).start()

    def accumulate(slab, block, panel):
        panel_high, panel_low = panel
        a = nt(high[slab], jnp.concatenate([panel_high, panel_low], 0))
        b = nt(low[slab], panel_high)
        sums[block] += a[:, :TILE] + a[:, TILE:] + b

    def owned(q, c):
        return pl.ds(pl.multiple_of((q * 2 + c) * TILE, TILE), TILE)

    def send_pair(block, first):
        for q in range(first, 4):
            src = sums.at[block, owned(q, 1 - core), :]
            remote(src, pair.at[block, q], pair_send, pair_recv.at[block], (row, sibling)).start()

    def send_parts(block, first):
        arrived(pair.at[block, pl.ds(first, 4 - first)], pair_recv.at[block])
        for q in range(first, 4):
            sums[block, owned(q, core), :] += pair[block, q]

            @pl.when(q != y)
            def _():
                src = sums.at[block, owned(q, core), :]
                remote(src, parts.at[block, y], part_send, part_recv.at[block, y], (row, q * 2 + core)).start()

    def own_points():
        return feat_ref[:, pl.ds(pl.multiple_of(col * TILE, TILE), TILE)]

    @pl.when(row == 0)
    def root():
        def start_piece(n, carry):
            block, slab = n // SLABS, n % SLABS
            for t in range(4):
                src = factor_ref.at[
                    pl.ds(pl.multiple_of(block * TILE + t * SUB, SUB), SUB),
                    pl.ds(pl.multiple_of(slab * SLAB, SLAB), SLAB),
                ]
                send_piece(src, n, t, t)
            return carry

        lax.fori_loop(0, AHEAD, start_piece, 0)
        sums[...] = jnp.zeros_like(sums)

        def load(half, slab):
            return pltpu.make_async_copy(
                factor_ref.at[pl.ds(half * 512, 512), pl.ds(pl.multiple_of(slab * SLAB, SLAB), SLAB)],
                stage.at[slab % 2, pl.ds(half * 512, 512), :],
                stage_sem.at[half, slab % 2],
            )

        def product(half, begin, end):
            def one(slab, carry):
                if half == 0:
                    carry = lax.fori_loop(AHEAD + slab * 3, AHEAD + slab * 3 + 3, start_piece, carry)
                load(half, slab).wait()
                h, l = two_parts(stage[slab % 2, pl.ds(half * 512, 512), :])
                high[slab, pl.ds(half * 512, 512), :] = h
                low[slab, pl.ds(half * 512, 512), :] = l

                @pl.when(slab + 2 < SLABS)
                def _():
                    load(half, slab + 2).start()

                panel_high, panel_low = high[slab, :512], low[slab, :512]
                if half == 0:
                    total = nt(h, panel_high * 0.5) + nt(h, panel_low)
                else:
                    total = nt(h, panel_high) + nt(h, panel_low) + nt(l, panel_high)
                for block in range(4):
                    sums[block, pl.ds(half * 512, 512), :] += total[:, block * TILE : (block + 1) * TILE]
                return carry

            lax.fori_loop(begin, end, one, 0)

        for half in range(2):
            load(half, 0).start()
            load(half, 1).start()
        product(0, 0, SLABS)
        for t in range(4):
            half = pl.ds(pl.multiple_of(core * (B // 2), TILE), B // 2)
            send_features(feat_ref.at[pl.ds(32 * t, 40), half], t, t)
        for n, (i, j) in enumerate(BLOCKS):
            gram[pl.ds(n * TILE, TILE), :] = sums[j, pl.ds(i * TILE, TILE), :] + sums[i, pl.ds(j * TILE, TILE), :].T
        mine = pl.ds(pl.multiple_of(col * SHARE, SHARE), SHARE)
        for peer in peers:
            src = gram.at[pl.ds(pl.multiple_of(peer * SHARE, SHARE), SHARE), :]
            remote(src, gram_parts.at[col], gram_send.at[0], gram_recv.at[0, col], (row, peer)).start()
        product(1, 0, 4)
        share = gram[mine, :]
        for peer in peers:
            arrived(gram_parts.at[peer], gram_recv.at[0, peer])
            share = share + gram_parts[peer]
        gram_all[mine, :] = share
        for peer in peers:
            remote(
                gram_all.at[mine, :], gram_all.at[mine, :], gram_send.at[1], gram_recv.at[1, col], (row, peer)
            ).start()
        for j in range(4):
            size = (4 - j) * TILE
            values = covariance(feat_ref[:, j * TILE : B], feat_ref[:, j * TILE : (j + 1) * TILE])
            same = lax.broadcasted_iota(jnp.int32, (size, TILE), 0) == lax.broadcasted_iota(jnp.int32, (size, TILE), 1)
            lower[pl.ds(COLUMN[j], size), :] = values + jnp.where(same, RIDGE, 0.0)
        for peer in peers:
            arrived(gram_all.at[pl.ds(pl.multiple_of(peer * SHARE, SHARE), SHARE), :], gram_recv.at[1, peer])
        lower[...] = lower[...] - gram_all[...]

        def at(i, j):
            return pl.ds(PLACE[i, j] * TILE, TILE)

        for j in range(4):
            tile[...] = lower[at(j, j), :]
            invert_factor(tile)
            inverse = tile[...]
            lower[at(j, j), :] = inverse
            for i in range(j + 1, 4):
                lower[at(i, j), :] = nt(lower[at(i, j), :], inverse, HIGHEST)
            for t in range(4):
                send_low(j, t, t)
            for k in range(j + 1, 4):
                for i in range(k, 4):
                    lower[at(i, k), :] = lower[at(i, k), :] - nt(lower[at(i, j), :], lower[at(k, j), :], HIGHEST)
        product(1, 4, SLABS)
        for block in range(4):
            send_pair(block, 2)
        slab_kernel[...] = covariance(own_points(), feat_ref[:, :B])
        for block in range(4):
            send_parts(block, 2)

    @pl.when(row != 0)
    def others():
        def load(slab):
            return pltpu.make_async_copy(
                factor_ref.at[:, pl.ds(pl.multiple_of(slab * SLAB, SLAB), SLAB)],
                stage.at[slab % 2],
                stage_sem.at[0, slab % 2],
            )

        load(0).start()
        load(1).start()
        sums[...] = jnp.zeros_like(sums)

        def slot(s, carry):
            for t in range(4):
                item = s - lags[t]

                @pl.when((item >= 0) & (item < PIECES))
                def _():
                    arrived(piece_at(item, t), piece_recv.at[item, t])
                    for d in range(4):
                        @pl.when(sends[t][d] == 1)
                        def _():
                            send_piece(piece_at(item, t), item, t, d)

                @pl.when((item >= PIECES) & (item < ITEMS))
                def _():
                    @pl.when(item == PIECES)
                    def _():
                        arrived(feat_at(t, core), feat_recv.at[t])
                        for d in range(4):
                            @pl.when(sends[t][d] == 1)
                            def _():
                                send_features(feat_at(t, core), t, d)
                        exchange(feat_at(t, core), 4, t)

                    for j in range(4):
                        @pl.when(item == PIECES + 1 + j)
                        def _():
                            arrived(low_at(j, t, core), low_recv.at[j, t])
                            for d in range(4):
                                @pl.when(sends[t][d] == 1)
                                def _():
                                    send_low(j, t, d)
                            exchange(low_at(j, t, core), j, t)

            @pl.when(s < SLABS)
            def _():
                load(s).wait()
                h, l = two_parts(stage[s % 2])
                high[s] = h
                low[s] = l

                @pl.when(s + 2 < SLABS)
                def _():
                    load(s + 2).start()

            m = s - last

            @pl.when(m == PIECES)
            def _():
                send_parts(3, 0)

            @pl.when(m == PIECES + 2)
            def _():
                for t in range(4):
                    arrived(feat_at(t, 1 - core), share_recv.at[4, t])
                anchors = jnp.concatenate([feat_land[t, :32] for t in range(3)] + [feat_land[3]], 0)
                slab_kernel[...] = covariance(own_points(), anchors)

            @pl.when((m >= 0) & (m < PIECES))
            def _():
                block, slab = m // SLABS, m % SLABS
                accumulate(slab, block, two_parts(land[m]))

                @pl.when(slab == SLABS - 1)
                def _():
                    send_pair(block, 0)

                @pl.when((slab == 1) & (block > 0))
                def _():
                    send_parts(block - 1, 0)

            return carry

        lax.fori_loop(0, ITEMS + last, slot, 0)

    solved = []
    rows = lax.broadcasted_iota(jnp.int32, (TILE, TILE), 0) + row * ROWS + col * TILE
    columns = lax.broadcasted_iota(jnp.int32, (TILE, TILE), 1)

    def rest(j):
        @pl.when(row != 0)
        def _():
            for t in range(4):
                arrived(low_at(j, t, 1 - core), share_recv.at[j, t])

        value = slab_kernel[:, j * TILE : (j + 1) * TILE]
        value = value + jnp.where(rows == columns + j * TILE, RIDGE, 0.0)
        for i in range(j):
            value = value - nt(solved[i], lower[pl.ds(PLACE[j, i] * TILE, TILE), :], HIGHEST)
        return value

    def solve(j, value):
        @pl.when(pivot)
        def _():
            place = COLUMN[j] + jnp.maximum(col - j, 0) * TILE
            own[...] = gram_all[pl.ds(pl.multiple_of(place, TILE), TILE), :]

        @pl.when(jnp.logical_not(pivot))
        def _():
            own[...] = sums[j, owned(y, core), :]
            for n in range(1, 4):
                other = (y + n) % 4
                arrived(parts.at[j, other], part_recv.at[j, other])
                own[...] += parts[j, other]

        value = nt(value - own[...], lower[pl.ds(PLACE[j, j] * TILE, TILE), :], HIGHEST)
        value = jnp.where(pivot & (col < j), 0.0, value)
        solved.append(value)
        out_ref[:, j * TILE : (j + 1) * TILE] = value

    for j in range(4):
        solve(j, rest(j))

    @pl.when(row != 0)
    def _():
        arrived(feat_land.at[:, :, pl.ds(0, B // 2)], share_send)
        arrived(lower.at[pl.ds(0, 5 * TILE), :], share_send)
        arrived(pair, pair_send)
        arrived(parts.at[:, pl.ds(0, 3)], part_send)

    @pl.when(row == 0)
    def _():
        arrived(pair.at[:, pl.ds(0, 2)], pair_send)

        @pl.when(pivot)
        def _():
            arrived(parts.at[:, pl.ds(0, 2)], part_send)

        @pl.when(jnp.logical_not(pivot))
        def _():
            arrived(parts.at[:, 0], part_send)

    for t in range(4):
        for d in range(4):
            @pl.when(sends[t][d] == 1)
            def _():
                arrived(land.at[:, pl.ds(0, SUB), :], piece_send.at[t, d])
                arrived(feat_at(t, 0), feat_send.at[t, d])
                arrived(lower.at[pl.ds(0, 5 * SUB), :], low_send.at[t, d])

    @pl.when(row == 0)
    def _():
        for phase in range(2):
            arrived(gram_parts.at[pl.ds(0, 7)], gram_send.at[phase])


def on_device(features, factor):
    dma = pltpu.SemaphoreType.DMA
    return pl.pallas_call(
        body,
        out_shape=jax.ShapeDtypeStruct((TILE, B), F32),
        in_specs=[pl.BlockSpec(memory_space=pltpu.VMEM), pl.BlockSpec(memory_space=pl.ANY)],
        out_specs=pl.BlockSpec(memory_space=pltpu.VMEM),
        scratch_shapes=[
            pltpu.VMEM((2, ROWS, SLAB), F32),
            pltpu.VMEM((SLABS, ROWS, SLAB), BF16),
            pltpu.VMEM((SLABS, ROWS, SLAB), BF16),
            pltpu.VMEM((PIECES, TILE, SLAB), F32),
            pltpu.VMEM((4, 40, B), F32),
            pltpu.VMEM((4, ROWS, TILE), F32),
            pltpu.VMEM((4, 4, TILE, TILE), F32),
            pltpu.VMEM((4, 4, TILE, TILE), F32),
            pltpu.VMEM((TILE, TILE), F32),
            pltpu.VMEM((10 * TILE, TILE), F32),
            pltpu.VMEM((8, SHARE, TILE), F32),
            pltpu.VMEM((10 * TILE, TILE), F32),
            pltpu.VMEM((10 * TILE, TILE), F32),
            pltpu.VMEM((TILE, TILE), F32),
            pltpu.VMEM((TILE, B), F32),
            dma((2, 2)),
            dma((4, 4)),
            dma((PIECES, 4)),
            dma((4, 4)),
            dma((4,)),
            dma((4, 4)),
            dma((4, 4)),
            dma,
            dma((4,)),
            dma,
            dma((4, 4)),
            dma((2,)),
            dma((2, 8)),
            dma,
            dma((5, 4)),
        ],
        compiler_params=pltpu.CompilerParams(
            collective_id=0, has_side_effects=True, vmem_limit_bytes=56 << 20
        ),
    )(features, factor)


def solution(mesh):
    placed = (P(None, "row"), P("row", "col"))
    return jax.shard_map(
        on_device, mesh=mesh, in_specs=placed, out_specs=P(("row", "col"), None), check_vma=False
    )
```

```python
import functools

import jax
import jax.numpy as jnp
from jax import lax
from jax.experimental import pallas as pl
from jax.experimental.pallas import tpu as pltpu
from jax.sharding import PartitionSpec as P

MESH = pl.DeviceIdType.MESH
HIGHEST = lax.Precision.HIGHEST
F32, BF16 = jnp.float32, jnp.bfloat16

B = 512
FEAT = 136
RIDGE = 40.0
TILE = 128
STRIP = 16
ROWS = 1024
SLAB = 512
SLABS = 8
PIECES = 32
SUB = 32
AHEAD = 8
ITEMS = PIECES + 1 + 4

TREES = (
    (1, 48, 64, 48, 27, 39, 53, 36, 41, 49, 65, 49, 48, 64, 80, 64),
    (2, 23, 35, 48, 48, 40, 50, 64, 64, 58, 66, 80, 48, 46, 50, 64),
    (4, 48, 64, 48, 48, 64, 80, 64, 38, 52, 68, 52, 30, 33, 53, 45),
    (8, 48, 44, 29, 48, 64, 56, 43, 64, 80, 72, 58, 48, 64, 56, 34),
)
BLOCKS = [(i, j) for j in range(4) for i in range(j, 4)]
PLACE = {b: n for n, b in enumerate(BLOCKS)}
COLUMN = [PLACE[j, j] * TILE for j in range(4)]
SHARE = len(BLOCKS) * TILE // 8


def lag(depth):
    return depth * 3 - 1


def pick(index, table):
    value = jnp.int32(0)
    for n, entry in enumerate(table):
        value = value + jnp.where(index == n, jnp.int32(entry), jnp.int32(0))
    return value


def nt(a, b, precision=None):
    return lax.dot_general(
        a, b, (((1,), (1,)), ((), ())), precision=precision, preferred_element_type=F32
    )


def tn(a, b, precision=None):
    return lax.dot_general(
        a, b, (((0,), (0,)), ((), ())), precision=precision, preferred_element_type=F32
    )


def two_parts(x):
    high = x.astype(BF16)
    return high, (x - high.astype(F32)).astype(BF16)


def three_parts(x):
    high = x.astype(BF16)
    rest = x - high.astype(F32)
    middle = rest.astype(BF16)
    return high, middle, (rest - middle.astype(F32)).astype(BF16)


def covariance(points, anchors):
    products = tn(points, anchors, HIGHEST)
    norm_points = tn(points * points, jnp.ones((FEAT, TILE), F32), HIGHEST)[:, :1]
    norm_anchors = jnp.sum(anchors * anchors, axis=0, keepdims=True)
    distance = norm_points + norm_anchors - 2.0 * products
    return products * (1.0 / FEAT) + jnp.exp(distance * (-0.5 / FEAT))


def invert_factor(t_ref):
    ri = lax.broadcasted_iota(jnp.int32, (STRIP, TILE), 0)
    ci = lax.broadcasted_iota(jnp.int32, (STRIP, TILE), 1)
    rj = lax.broadcasted_iota(jnp.int32, (TILE, TILE), 0)
    cj = lax.broadcasted_iota(jnp.int32, (TILE, TILE), 1)

    def strip(k, carry):
        first = pl.multiple_of(k * STRIP, STRIP)
        rows = t_ref[pl.ds(first, STRIP), :]
        turned = pltpu.roll(rows, TILE - first, 1)
        cols = [jnp.broadcast_to(turned[:, c : c + 1], (STRIP, TILE)) for c in range(STRIP)]
        rows = jnp.where((ci >= first) & (ci < first + STRIP), (ci - first == ri).astype(F32), rows)
        pivots = jnp.ones((STRIP, TILE), F32)
        for c in range(STRIP):
            pivot = jnp.broadcast_to(cols[c][c : c + 1, :], (STRIP, TILE))
            pivots = jnp.where(ri == c, pivot, pivots)
            factor = jnp.where(ri > c, cols[c] * (1.0 / pivot), 0.0)
            for d in range(c + 1, STRIP):
                cols[d] = cols[d] - factor * cols[d][c : c + 1, :]
            rows = rows - factor * rows[c : c + 1, :]
        scale = lax.rsqrt(pivots)
        scale = scale * (1.5 - 0.5 * pivots * scale * scale)
        rows = rows * scale
        lh, lm, ll = three_parts(jnp.where(ci >= first + STRIP, rows, 0.0))
        rh, rm, rl = three_parts(rows)
        change = tn(
            jnp.concatenate([lh, lh, lm, lh, lm, ll], 0),
            jnp.concatenate([rh, rm, rh, rl, rm, rh], 0),
        )
        below = (cj >= first) & (cj < first + STRIP) & (rj >= first + STRIP)
        t_ref[...] = jnp.where(below, 0.0, t_ref[...]) - change
        t_ref[pl.ds(first, STRIP), :] = jnp.where(ci < first + STRIP, rows, 0.0)
        return carry

    lax.fori_loop(0, TILE // STRIP, strip, 0)


def body(
    feat_ref, factor_ref, out_ref,
    stage, high, low, land, feat_land, sums, pair, parts, own, gram, gram_parts, gram_all, lower, tile, slab_kernel,
    points, pivots, points_sem, stage_sem, piece_send, piece_recv, feat_send, feat_recv, low_send, low_recv,
    pair_send, pair_recv, part_send, part_recv, gram_send, gram_recv, share_send, share_recv,
):
    row, col = lax.axis_index("row"), lax.axis_index("col")
    x, z = row // 4, row % 4
    near = [((x + 1) % 4) * 4 + z, x * 4 + (z + 1) % 4, ((x + 3) % 4) * 4 + z, x * 4 + (z + 3) % 4]
    codes = [pick(row, table) for table in TREES]
    depth = [code // 16 for code in codes]
    sends = [[(code // (1 << d)) % 2 for d in range(4)] for code in codes]
    peers = [(col + n) % 8 for n in range(1, 8)]
    y, core = col // 2, col % 2
    sibling = y * 2 + 1 - core
    pivot = (row == 0) & (col < 4)
    lags = [lag(d) for d in depth]
    last = jnp.maximum(jnp.maximum(lags[0], lags[1]), jnp.maximum(lags[2], lags[3]))

    barrier = pltpu.get_barrier_semaphore()
    for d in range(4):
        pl.semaphore_signal(barrier, inc=1, device_id=(near[d], col), device_id_type=MESH)
    for peer in peers:
        pl.semaphore_signal(barrier, inc=1, device_id=(row, peer), device_id_type=MESH)
    pl.semaphore_wait(barrier, 11)

    def remote(src, dst, send, recv, device):
        return pltpu.make_async_remote_copy(
            src_ref=src, dst_ref=dst, send_sem=send, recv_sem=recv, device_id=device, device_id_type=MESH
        )

    def arrived(ref, sem):
        pltpu.make_async_copy(ref, ref, sem).wait()

    def piece_at(n, t):
        return land.at[n, pl.ds(t * SUB, SUB), :]

    def low_at(j, t, c):
        size = SUB // 2 * (4 - j)
        return lower.at[pl.ds(pl.multiple_of(COLUMN[j] + (2 * t + c) * size, 16), size), :]

    def feat_at(t, c):
        return feat_land.at[t, :, pl.ds(pl.multiple_of(c * (B // 2), TILE), B // 2)]

    def exchange(ref, item, t):
        remote(ref, ref, share_send, share_recv.at[item, t], (row, sibling)).start()

    def send_piece(src, n, t, d):
        remote(src, piece_at(n, t), piece_send.at[t, d], piece_recv.at[n, t], (near[d], col)).start()

    def send_features(src, t, d):
        remote(src, feat_at(t, core), feat_send.at[t, d], feat_recv.at[t], (near[d], col)).start()

    def send_low(j, t, d):
        remote(low_at(j, t, core), low_at(j, t, core), low_send.at[t, d], low_recv.at[j, t], (near[d], col)).start()

    def accumulate(slab, block, panel):
        panel_high, panel_low = panel
        a = nt(high[slab], jnp.concatenate([panel_high, panel_low], 0))
        b = nt(low[slab], panel_high)
        sums[block] += a[:, :TILE] + a[:, TILE:] + b

    def owned(q, c):
        return pl.ds(pl.multiple_of((q * 2 + c) * TILE, TILE), TILE)

    def send_pair(block, first):
        for q in range(first, 4):
            src = sums.at[block, owned(q, 1 - core), :]
            remote(src, pair.at[block, q], pair_send, pair_recv.at[block], (row, sibling)).start()

    def send_parts(block, first):
        arrived(pair.at[block, pl.ds(first, 4 - first)], pair_recv.at[block])
        for q in range(first, 4):
            sums[block, owned(q, core), :] += pair[block, q]

            @pl.when(q != y)
            def _():
                src = sums.at[block, owned(q, core), :]
                remote(src, parts.at[block, y], part_send, part_recv.at[block, y], (row, q * 2 + core)).start()

    own_points = pltpu.make_async_copy(
        feat_ref.at[:, pl.ds(pl.multiple_of(col * TILE, TILE), TILE)], points, points_sem.at[0]
    )
    own_points.start()

    @pl.when(row == 0)
    def root():
        def start_piece(n, carry):
            block, slab = n // SLABS, n % SLABS
            for t in range(4):
                src = factor_ref.at[
                    pl.ds(pl.multiple_of(block * TILE + t * SUB, SUB), SUB),
                    pl.ds(pl.multiple_of(slab * SLAB, SLAB), SLAB),
                ]
                send_piece(src, n, t, t)
            return carry

        lax.fori_loop(0, AHEAD, start_piece, 0)
        sums[...] = jnp.zeros_like(sums)

        def load(half, slab):
            return pltpu.make_async_copy(
                factor_ref.at[pl.ds(half * 512, 512), pl.ds(pl.multiple_of(slab * SLAB, SLAB), SLAB)],
                stage.at[slab % 2, pl.ds(half * 512, 512), :],
                stage_sem.at[half, slab % 2],
            )

        def product(half, begin, end):
            def one(slab, carry):
                if half == 0:
                    carry = lax.fori_loop(AHEAD + slab * 3, AHEAD + slab * 3 + 3, start_piece, carry)
                load(half, slab).wait()
                h, l = two_parts(stage[slab % 2, pl.ds(half * 512, 512), :])
                high[slab, pl.ds(half * 512, 512), :] = h
                low[slab, pl.ds(half * 512, 512), :] = l

                @pl.when(slab + 2 < SLABS)
                def _():
                    load(half, slab + 2).start()

                panel_high, panel_low = high[slab, :512], low[slab, :512]
                if half == 0:
                    total = nt(h, panel_high * 0.5) + nt(h, panel_low)
                else:
                    total = nt(h, panel_high) + nt(h, panel_low) + nt(l, panel_high)
                for block in range(4):
                    sums[block, pl.ds(half * 512, 512), :] += total[:, block * TILE : (block + 1) * TILE]
                return carry

            lax.fori_loop(begin, end, one, 0)

        pivot_points = pltpu.make_async_copy(feat_ref.at[:, pl.ds(0, B)], pivots, points_sem.at[1])
        pivot_points.start()
        for half in range(2):
            load(half, 0).start()
            load(half, 1).start()
        product(0, 0, SLABS)
        for t in range(4):
            half = pl.ds(pl.multiple_of(core * (B // 2), TILE), B // 2)
            send_features(feat_ref.at[pl.ds(32 * t, 40), half], t, t)
        for n, (i, j) in enumerate(BLOCKS):
            gram[pl.ds(n * TILE, TILE), :] = sums[j, pl.ds(i * TILE, TILE), :] + sums[i, pl.ds(j * TILE, TILE), :].T
        mine = pl.ds(pl.multiple_of(col * SHARE, SHARE), SHARE)
        for peer in peers:
            src = gram.at[pl.ds(pl.multiple_of(peer * SHARE, SHARE), SHARE), :]
            remote(src, gram_parts.at[col], gram_send.at[0], gram_recv.at[0, col], (row, peer)).start()
        product(1, 0, 4)
        share = gram[mine, :]
        for peer in peers:
            arrived(gram_parts.at[peer], gram_recv.at[0, peer])
            share = share + gram_parts[peer]
        gram_all[mine, :] = share
        for peer in peers:
            remote(
                gram_all.at[mine, :], gram_all.at[mine, :], gram_send.at[1], gram_recv.at[1, col], (row, peer)
            ).start()
        pivot_points.wait()
        for j in range(4):
            size = (4 - j) * TILE
            values = covariance(pivots[:, j * TILE : B], pivots[:, j * TILE : (j + 1) * TILE])
            same = lax.broadcasted_iota(jnp.int32, (size, TILE), 0) == lax.broadcasted_iota(jnp.int32, (size, TILE), 1)
            lower[pl.ds(COLUMN[j], size), :] = values + jnp.where(same, RIDGE, 0.0)
        for peer in peers:
            arrived(gram_all.at[pl.ds(pl.multiple_of(peer * SHARE, SHARE), SHARE), :], gram_recv.at[1, peer])
        lower[...] = lower[...] - gram_all[...]

        def at(i, j):
            return pl.ds(PLACE[i, j] * TILE, TILE)

        for j in range(4):
            tile[...] = lower[at(j, j), :]
            invert_factor(tile)
            inverse = tile[...]
            lower[at(j, j), :] = inverse
            for i in range(j + 1, 4):
                lower[at(i, j), :] = nt(lower[at(i, j), :], inverse, HIGHEST)
            for t in range(4):
                send_low(j, t, t)
            for k in range(j + 1, 4):
                for i in range(k, 4):
                    lower[at(i, k), :] = lower[at(i, k), :] - nt(lower[at(i, j), :], lower[at(k, j), :], HIGHEST)
        product(1, 4, SLABS)
        for block in range(4):
            send_pair(block, 2)
        own_points.wait()
        slab_kernel[...] = covariance(points[...], pivots[...])
        for block in range(4):
            send_parts(block, 2)

    @pl.when(row != 0)
    def others():
        def load(slab):
            return pltpu.make_async_copy(
                factor_ref.at[:, pl.ds(pl.multiple_of(slab * SLAB, SLAB), SLAB)],
                stage.at[slab % 2],
                stage_sem.at[0, slab % 2],
            )

        load(0).start()
        load(1).start()
        sums[...] = jnp.zeros_like(sums)

        def slot(s, carry):
            for t in range(4):
                item = s - lags[t]

                @pl.when((item >= 0) & (item < PIECES))
                def _():
                    arrived(piece_at(item, t), piece_recv.at[item, t])
                    for d in range(4):
                        @pl.when(sends[t][d] == 1)
                        def _():
                            send_piece(piece_at(item, t), item, t, d)

                @pl.when((item >= PIECES) & (item < ITEMS))
                def _():
                    @pl.when(item == PIECES)
                    def _():
                        arrived(feat_at(t, core), feat_recv.at[t])
                        for d in range(4):
                            @pl.when(sends[t][d] == 1)
                            def _():
                                send_features(feat_at(t, core), t, d)
                        exchange(feat_at(t, core), 4, t)

                    for j in range(4):
                        @pl.when(item == PIECES + 1 + j)
                        def _():
                            arrived(low_at(j, t, core), low_recv.at[j, t])
                            for d in range(4):
                                @pl.when(sends[t][d] == 1)
                                def _():
                                    send_low(j, t, d)
                            exchange(low_at(j, t, core), j, t)

            @pl.when(s < SLABS)
            def _():
                load(s).wait()
                h, l = two_parts(stage[s % 2])
                high[s] = h
                low[s] = l

                @pl.when(s + 2 < SLABS)
                def _():
                    load(s + 2).start()

            m = s - last

            @pl.when(m == PIECES)
            def _():
                send_parts(3, 0)

            @pl.when(m == PIECES + 2)
            def _():
                for t in range(4):
                    arrived(feat_at(t, 1 - core), share_recv.at[4, t])
                anchors = jnp.concatenate([feat_land[t, :32] for t in range(3)] + [feat_land[3]], 0)
                own_points.wait()
                slab_kernel[...] = covariance(points[...], anchors)

            @pl.when((m >= 0) & (m < PIECES))
            def _():
                block, slab = m // SLABS, m % SLABS
                accumulate(slab, block, two_parts(land[m]))

                @pl.when(slab == SLABS - 1)
                def _():
                    send_pair(block, 0)

                @pl.when((slab == 1) & (block > 0))
                def _():
                    send_parts(block - 1, 0)

            return carry

        lax.fori_loop(0, ITEMS + last, slot, 0)

    solved = []
    rows = lax.broadcasted_iota(jnp.int32, (TILE, TILE), 0) + row * ROWS + col * TILE
    columns = lax.broadcasted_iota(jnp.int32, (TILE, TILE), 1)

    def rest(j):
        @pl.when(row != 0)
        def _():
            for t in range(4):
                arrived(low_at(j, t, 1 - core), share_recv.at[j, t])

        value = slab_kernel[:, j * TILE : (j + 1) * TILE]
        value = value + jnp.where(rows == columns + j * TILE, RIDGE, 0.0)
        for i in range(j):
            value = value - nt(solved[i], lower[pl.ds(PLACE[j, i] * TILE, TILE), :], HIGHEST)
        return value

    def solve(j, value):
        @pl.when(pivot)
        def _():
            place = COLUMN[j] + jnp.maximum(col - j, 0) * TILE
            own[...] = gram_all[pl.ds(pl.multiple_of(place, TILE), TILE), :]

        @pl.when(jnp.logical_not(pivot))
        def _():
            own[...] = sums[j, owned(y, core), :]
            for n in range(1, 4):
                other = (y + n) % 4
                arrived(parts.at[j, other], part_recv.at[j, other])
                own[...] += parts[j, other]

        value = nt(value - own[...], lower[pl.ds(PLACE[j, j] * TILE, TILE), :], HIGHEST)
        value = jnp.where(pivot & (col < j), 0.0, value)
        solved.append(value)
        out_ref[:, j * TILE : (j + 1) * TILE] = value

    for j in range(4):
        solve(j, rest(j))

    @pl.when(row != 0)
    def _():
        arrived(feat_land.at[:, :, pl.ds(0, B // 2)], share_send)
        arrived(lower.at[pl.ds(0, 5 * TILE), :], share_send)
        arrived(pair, pair_send)
        arrived(parts.at[:, pl.ds(0, 3)], part_send)

    @pl.when(row == 0)
    def _():
        arrived(pair.at[:, pl.ds(0, 2)], pair_send)

        @pl.when(pivot)
        def _():
            arrived(parts.at[:, pl.ds(0, 2)], part_send)

        @pl.when(jnp.logical_not(pivot))
        def _():
            arrived(parts.at[:, 0], part_send)

    for t in range(4):
        for d in range(4):
            @pl.when(sends[t][d] == 1)
            def _():
                arrived(land.at[:, pl.ds(0, SUB), :], piece_send.at[t, d])
                arrived(feat_at(t, 0), feat_send.at[t, d])
                arrived(lower.at[pl.ds(0, 5 * SUB), :], low_send.at[t, d])

    @pl.when(row == 0)
    def _():
        for phase in range(2):
            arrived(gram_parts.at[pl.ds(0, 7)], gram_send.at[phase])


def on_device(features, factor):
    dma = pltpu.SemaphoreType.DMA
    return pl.pallas_call(
        body,
        out_shape=pltpu.VMEM((TILE, B), F32),
        in_specs=[pl.BlockSpec(memory_space=pl.ANY)] * 2,
        out_specs=pl.BlockSpec(memory_space=pltpu.VMEM),
        scratch_shapes=[
            pltpu.VMEM((2, ROWS, SLAB), F32),
            pltpu.VMEM((SLABS, ROWS, SLAB), BF16),
            pltpu.VMEM((SLABS, ROWS, SLAB), BF16),
            pltpu.VMEM((PIECES, TILE, SLAB), F32),
            pltpu.VMEM((4, 40, B), F32),
            pltpu.VMEM((4, ROWS, TILE), F32),
            pltpu.VMEM((4, 4, TILE, TILE), F32),
            pltpu.VMEM((4, 4, TILE, TILE), F32),
            pltpu.VMEM((TILE, TILE), F32),
            pltpu.VMEM((10 * TILE, TILE), F32),
            pltpu.VMEM((8, SHARE, TILE), F32),
            pltpu.VMEM((10 * TILE, TILE), F32),
            pltpu.VMEM((10 * TILE, TILE), F32),
            pltpu.VMEM((TILE, TILE), F32),
            pltpu.VMEM((TILE, B), F32),
            pltpu.VMEM((FEAT, TILE), F32),
            pltpu.VMEM((FEAT, B), F32),
            dma((2,)),
            dma((2, 2)),
            dma((4, 4)),
            dma((PIECES, 4)),
            dma((4, 4)),
            dma((4,)),
            dma((4, 4)),
            dma((4, 4)),
            dma,
            dma((4,)),
            dma,
            dma((4, 4)),
            dma((2,)),
            dma((2, 8)),
            dma,
            dma((5, 4)),
        ],
        compiler_params=pltpu.CompilerParams(
            collective_id=0, has_side_effects=True, vmem_limit_bytes=56 << 20
        ),
    )(features, factor)


def solution(mesh):
    placed = (P(None, "row"), P("row", "col"))
    return jax.shard_map(
        on_device, mesh=mesh, in_specs=placed, out_specs=P(("row", "col"), None), check_vma=False
    )
```

```python
import functools

import jax
import jax.numpy as jnp
from jax import lax
from jax.experimental import pallas as pl
from jax.experimental.pallas import tpu as pltpu
from jax.sharding import PartitionSpec as P

MESH = pl.DeviceIdType.MESH
HIGHEST = lax.Precision.HIGHEST
F32, BF16 = jnp.float32, jnp.bfloat16

B = 512
FEAT = 136
RIDGE = 40.0
TILE = 128
STRIP = 16
ROWS = 1024
SLAB = 512
SLABS = 8
PIECES = 32
SUB = 32
AHEAD = 8
ITEMS = PIECES + 1 + 4

TREES = (
    (1, 48, 64, 48, 27, 39, 53, 36, 41, 49, 65, 49, 48, 64, 80, 64),
    (2, 23, 35, 48, 48, 40, 50, 64, 64, 58, 66, 80, 48, 46, 50, 64),
    (4, 48, 64, 48, 48, 64, 80, 64, 38, 52, 68, 52, 30, 33, 53, 45),
    (8, 48, 44, 29, 48, 64, 56, 43, 64, 80, 72, 58, 48, 64, 56, 34),
)
BLOCKS = [(i, j) for j in range(4) for i in range(j, 4)]
PLACE = {b: n for n, b in enumerate(BLOCKS)}
COLUMN = [PLACE[j, j] * TILE for j in range(4)]
SHARE = len(BLOCKS) * TILE // 8


def lag(depth):
    return depth * 7 // 2 - 1


def pick(index, table):
    value = jnp.int32(0)
    for n, entry in enumerate(table):
        value = value + jnp.where(index == n, jnp.int32(entry), jnp.int32(0))
    return value


def nt(a, b, precision=None):
    return lax.dot_general(
        a, b, (((1,), (1,)), ((), ())), precision=precision, preferred_element_type=F32
    )


def tn(a, b, precision=None):
    return lax.dot_general(
        a, b, (((0,), (0,)), ((), ())), precision=precision, preferred_element_type=F32
    )


def two_parts(x):
    high = x.astype(BF16)
    return high, (x - high.astype(F32)).astype(BF16)


def three_parts(x):
    high = x.astype(BF16)
    rest = x - high.astype(F32)
    middle = rest.astype(BF16)
    return high, middle, (rest - middle.astype(F32)).astype(BF16)


def covariance(points, anchors):
    products = tn(points, anchors, HIGHEST)
    norm_points = tn(points * points, jnp.ones((FEAT, TILE), F32), HIGHEST)[:, :1]
    norm_anchors = jnp.sum(anchors * anchors, axis=0, keepdims=True)
    distance = norm_points + norm_anchors - 2.0 * products
    return products * (1.0 / FEAT) + jnp.exp(distance * (-0.5 / FEAT))


def invert_factor(t_ref):
    ri = lax.broadcasted_iota(jnp.int32, (STRIP, TILE), 0)
    ci = lax.broadcasted_iota(jnp.int32, (STRIP, TILE), 1)
    rj = lax.broadcasted_iota(jnp.int32, (TILE, TILE), 0)
    cj = lax.broadcasted_iota(jnp.int32, (TILE, TILE), 1)

    def strip(k, carry):
        first = pl.multiple_of(k * STRIP, STRIP)
        rows = t_ref[pl.ds(first, STRIP), :]
        turned = pltpu.roll(rows, TILE - first, 1)
        cols = [jnp.broadcast_to(turned[:, c : c + 1], (STRIP, TILE)) for c in range(STRIP)]
        rows = jnp.where((ci >= first) & (ci < first + STRIP), (ci - first == ri).astype(F32), rows)
        pivots = jnp.ones((STRIP, TILE), F32)
        for c in range(STRIP):
            pivot = jnp.broadcast_to(cols[c][c : c + 1, :], (STRIP, TILE))
            pivots = jnp.where(ri == c, pivot, pivots)
            factor = jnp.where(ri > c, cols[c] * (1.0 / pivot), 0.0)
            for d in range(c + 1, STRIP):
                cols[d] = cols[d] - factor * cols[d][c : c + 1, :]
            rows = rows - factor * rows[c : c + 1, :]
        scale = lax.rsqrt(pivots)
        scale = scale * (1.5 - 0.5 * pivots * scale * scale)
        rows = rows * scale
        lh, lm, ll = three_parts(jnp.where(ci >= first + STRIP, rows, 0.0))
        rh, rm, rl = three_parts(rows)
        change = tn(
            jnp.concatenate([lh, lh, lm, lh, lm, ll], 0),
            jnp.concatenate([rh, rm, rh, rl, rm, rh], 0),
        )
        below = (cj >= first) & (cj < first + STRIP) & (rj >= first + STRIP)
        t_ref[...] = jnp.where(below, 0.0, t_ref[...]) - change
        t_ref[pl.ds(first, STRIP), :] = jnp.where(ci < first + STRIP, rows, 0.0)
        return carry

    lax.fori_loop(0, TILE // STRIP, strip, 0)


def body(
    feat_ref, factor_ref, out_ref,
    stage, high, low, land, feat_land, sums, pair, parts, own, gram, gram_parts, gram_all, lower, tile, slab_kernel,
    points, pivots, points_sem, stage_sem, piece_send, piece_recv, feat_send, feat_recv, low_send, low_recv,
    pair_send, pair_recv, part_send, part_recv, gram_send, gram_recv, share_send, share_recv,
):
    row, col = lax.axis_index("row"), lax.axis_index("col")
    x, z = row // 4, row % 4
    near = [((x + 1) % 4) * 4 + z, x * 4 + (z + 1) % 4, ((x + 3) % 4) * 4 + z, x * 4 + (z + 3) % 4]
    codes = [pick(row, table) for table in TREES]
    depth = [code // 16 for code in codes]
    sends = [[(code // (1 << d)) % 2 for d in range(4)] for code in codes]
    peers = [(col + n) % 8 for n in range(1, 8)]
    y, core = col // 2, col % 2
    sibling = y * 2 + 1 - core
    pivot = (row == 0) & (col < 4)
    lags = [lag(d) for d in depth]
    last = jnp.maximum(jnp.maximum(lags[0], lags[1]), jnp.maximum(lags[2], lags[3]))

    barrier = pltpu.get_barrier_semaphore()
    for d in range(4):
        pl.semaphore_signal(barrier, inc=1, device_id=(near[d], col), device_id_type=MESH)
    for peer in peers:
        pl.semaphore_signal(barrier, inc=1, device_id=(row, peer), device_id_type=MESH)
    pl.semaphore_wait(barrier, 11)

    def remote(src, dst, send, recv, device):
        return pltpu.make_async_remote_copy(
            src_ref=src, dst_ref=dst, send_sem=send, recv_sem=recv, device_id=device, device_id_type=MESH
        )

    def arrived(ref, sem):
        pltpu.make_async_copy(ref, ref, sem).wait()

    def piece_at(n, t):
        return land.at[n, pl.ds(t * SUB, SUB), :]

    def low_at(j, t, c):
        size = SUB // 2 * (4 - j)
        return lower.at[pl.ds(pl.multiple_of(COLUMN[j] + (2 * t + c) * size, 16), size), :]

    def feat_at(t, c):
        return feat_land.at[t, :, pl.ds(pl.multiple_of(c * (B // 2), TILE), B // 2)]

    def exchange(ref, item, t):
        remote(ref, ref, share_send, share_recv.at[item, t], (row, sibling)).start()

    def send_piece(src, n, t, d):
        remote(src, piece_at(n, t), piece_send.at[t, d], piece_recv.at[n, t], (near[d], col)).start()

    def send_features(src, t, d):
        remote(src, feat_at(t, core), feat_send.at[t, d], feat_recv.at[t], (near[d], col)).start()

    def send_low(j, t, d):
        remote(low_at(j, t, core), low_at(j, t, core), low_send.at[t, d], low_recv.at[j, t], (near[d], col)).start()

    def accumulate(slab, block, panel):
        panel_high, panel_low = panel
        a = nt(high[slab], jnp.concatenate([panel_high, panel_low], 0))
        b = nt(low[slab], panel_high)
        sums[block] += a[:, :TILE] + a[:, TILE:] + b

    def owned(q, c):
        return pl.ds(pl.multiple_of((q * 2 + c) * TILE, TILE), TILE)

    def send_pair(block, first):
        for q in range(first, 4):
            src = sums.at[block, owned(q, 1 - core), :]
            remote(src, pair.at[block, q], pair_send, pair_recv.at[block], (row, sibling)).start()

    def send_parts(block, first):
        arrived(pair.at[block, pl.ds(first, 4 - first)], pair_recv.at[block])
        for q in range(first, 4):
            sums[block, owned(q, core), :] += pair[block, q]

            @pl.when(q != y)
            def _():
                src = sums.at[block, owned(q, core), :]
                remote(src, parts.at[block, y], part_send, part_recv.at[block, y], (row, q * 2 + core)).start()

    own_points = pltpu.make_async_copy(
        feat_ref.at[:, pl.ds(pl.multiple_of(col * TILE, TILE), TILE)], points, points_sem.at[0]
    )
    own_points.start()

    @pl.when(row == 0)
    def root():
        def start_piece(n, carry):
            block, slab = n // SLABS, n % SLABS
            for t in range(4):
                src = factor_ref.at[
                    pl.ds(pl.multiple_of(block * TILE + t * SUB, SUB), SUB),
                    pl.ds(pl.multiple_of(slab * SLAB, SLAB), SLAB),
                ]
                send_piece(src, n, t, t)
            return carry

        lax.fori_loop(0, AHEAD, start_piece, 0)
        sums[...] = jnp.zeros_like(sums)

        def load(half, slab):
            return pltpu.make_async_copy(
                factor_ref.at[pl.ds(half * 512, 512), pl.ds(pl.multiple_of(slab * SLAB, SLAB), SLAB)],
                stage.at[slab % 2, pl.ds(half * 512, 512), :],
                stage_sem.at[half, slab % 2],
            )

        def product(half, begin, end):
            def one(slab, carry):
                if half == 0:
                    carry = lax.fori_loop(AHEAD + slab * 3, AHEAD + slab * 3 + 3, start_piece, carry)
                load(half, slab).wait()
                h, l = two_parts(stage[slab % 2, pl.ds(half * 512, 512), :])
                high[slab, pl.ds(half * 512, 512), :] = h
                low[slab, pl.ds(half * 512, 512), :] = l

                @pl.when(slab + 2 < SLABS)
                def _():
                    load(half, slab + 2).start()

                panel_high, panel_low = high[slab, :512], low[slab, :512]
                if half == 0:
                    total = nt(h, panel_high * 0.5) + nt(h, panel_low)
                else:
                    total = nt(h, panel_high) + nt(h, panel_low) + nt(l, panel_high)
                for block in range(4):
                    sums[block, pl.ds(half * 512, 512), :] += total[:, block * TILE : (block + 1) * TILE]
                return carry

            lax.fori_loop(begin, end, one, 0)

        pivot_points = pltpu.make_async_copy(feat_ref.at[:, pl.ds(0, B)], pivots, points_sem.at[1])
        pivot_points.start()
        for half in range(2):
            load(half, 0).start()
            load(half, 1).start()
        product(0, 0, SLABS)
        for t in range(4):
            half = pl.ds(pl.multiple_of(core * (B // 2), TILE), B // 2)
            send_features(feat_ref.at[pl.ds(32 * t, 40), half], t, t)
        for n, (i, j) in enumerate(BLOCKS):
            gram[pl.ds(n * TILE, TILE), :] = sums[j, pl.ds(i * TILE, TILE), :] + sums[i, pl.ds(j * TILE, TILE), :].T
        mine = pl.ds(pl.multiple_of(col * SHARE, SHARE), SHARE)
        for peer in peers:
            src = gram.at[pl.ds(pl.multiple_of(peer * SHARE, SHARE), SHARE), :]
            remote(src, gram_parts.at[col], gram_send.at[0], gram_recv.at[0, col], (row, peer)).start()
        product(1, 0, 4)
        share = gram[mine, :]
        for peer in peers:
            arrived(gram_parts.at[peer], gram_recv.at[0, peer])
            share = share + gram_parts[peer]
        gram_all[mine, :] = share
        for peer in peers:
            remote(
                gram_all.at[mine, :], gram_all.at[mine, :], gram_send.at[1], gram_recv.at[1, col], (row, peer)
            ).start()
        pivot_points.wait()
        for j in range(4):
            size = (4 - j) * TILE
            values = covariance(pivots[:, j * TILE : B], pivots[:, j * TILE : (j + 1) * TILE])
            same = lax.broadcasted_iota(jnp.int32, (size, TILE), 0) == lax.broadcasted_iota(jnp.int32, (size, TILE), 1)
            lower[pl.ds(COLUMN[j], size), :] = values + jnp.where(same, RIDGE, 0.0)
        for peer in peers:
            arrived(gram_all.at[pl.ds(pl.multiple_of(peer * SHARE, SHARE), SHARE), :], gram_recv.at[1, peer])
        lower[...] = lower[...] - gram_all[...]

        def at(i, j):
            return pl.ds(PLACE[i, j] * TILE, TILE)

        for j in range(4):
            tile[...] = lower[at(j, j), :]
            invert_factor(tile)
            inverse = tile[...]
            lower[at(j, j), :] = inverse
            for i in range(j + 1, 4):
                lower[at(i, j), :] = nt(lower[at(i, j), :], inverse, HIGHEST)
            for t in range(4):
                send_low(j, t, t)
            for k in range(j + 1, 4):
                for i in range(k, 4):
                    lower[at(i, k), :] = lower[at(i, k), :] - nt(lower[at(i, j), :], lower[at(k, j), :], HIGHEST)
        product(1, 4, SLABS)
        for block in range(4):
            send_pair(block, 2)
        own_points.wait()
        slab_kernel[...] = covariance(points[...], pivots[...])
        for block in range(4):
            send_parts(block, 2)

    @pl.when(row != 0)
    def others():
        def load(slab):
            return pltpu.make_async_copy(
                factor_ref.at[:, pl.ds(pl.multiple_of(slab * SLAB, SLAB), SLAB)],
                stage.at[slab % 2],
                stage_sem.at[0, slab % 2],
            )

        load(0).start()
        load(1).start()
        sums[...] = jnp.zeros_like(sums)

        def slot(s, carry):
            @pl.when(s - last == PIECES)
            def _():
                send_parts(3, 0)

            for t in range(4):
                item = s - lags[t]

                @pl.when((item >= 0) & (item < PIECES))
                def _():
                    arrived(piece_at(item, t), piece_recv.at[item, t])
                    for d in range(4):
                        @pl.when(sends[t][d] == 1)
                        def _():
                            send_piece(piece_at(item, t), item, t, d)

                @pl.when((item >= PIECES) & (item < ITEMS))
                def _():
                    @pl.when(item == PIECES)
                    def _():
                        arrived(feat_at(t, core), feat_recv.at[t])
                        for d in range(4):
                            @pl.when(sends[t][d] == 1)
                            def _():
                                send_features(feat_at(t, core), t, d)
                        exchange(feat_at(t, core), 4, t)

                    for j in range(4):
                        @pl.when(item == PIECES + 1 + j)
                        def _():
                            arrived(low_at(j, t, core), low_recv.at[j, t])
                            for d in range(4):
                                @pl.when(sends[t][d] == 1)
                                def _():
                                    send_low(j, t, d)
                            exchange(low_at(j, t, core), j, t)

            @pl.when(s < SLABS)
            def _():
                load(s).wait()
                h, l = two_parts(stage[s % 2])
                high[s] = h
                low[s] = l

                @pl.when(s + 2 < SLABS)
                def _():
                    load(s + 2).start()

            m = s - last

            @pl.when(m == PIECES + 2)
            def _():
                for t in range(4):
                    arrived(feat_at(t, 1 - core), share_recv.at[4, t])
                anchors = jnp.concatenate([feat_land[t, :32] for t in range(3)] + [feat_land[3]], 0)
                own_points.wait()
                slab_kernel[...] = covariance(points[...], anchors)

            @pl.when((m >= 0) & (m < PIECES))
            def _():
                block, slab = m // SLABS, m % SLABS
                accumulate(slab, block, two_parts(land[m]))

                @pl.when(slab == SLABS - 1)
                def _():
                    send_pair(block, 0)

                @pl.when((slab == 1) & (block > 0))
                def _():
                    send_parts(block - 1, 0)

            return carry

        lax.fori_loop(0, ITEMS + last, slot, 0)

    solved = []
    rows = lax.broadcasted_iota(jnp.int32, (TILE, TILE), 0) + row * ROWS + col * TILE
    columns = lax.broadcasted_iota(jnp.int32, (TILE, TILE), 1)

    def rest(j):
        @pl.when(row != 0)
        def _():
            for t in range(4):
                arrived(low_at(j, t, 1 - core), share_recv.at[j, t])

        value = slab_kernel[:, j * TILE : (j + 1) * TILE]
        value = value + jnp.where(rows == columns + j * TILE, RIDGE, 0.0)
        for i in range(j):
            value = value - nt(solved[i], lower[pl.ds(PLACE[j, i] * TILE, TILE), :], HIGHEST)
        return value

    def solve(j, value):
        @pl.when(pivot)
        def _():
            place = COLUMN[j] + jnp.maximum(col - j, 0) * TILE
            own[...] = gram_all[pl.ds(pl.multiple_of(place, TILE), TILE), :]

        @pl.when(jnp.logical_not(pivot))
        def _():
            own[...] = sums[j, owned(y, core), :]
            for n in range(1, 4):
                other = (y + n) % 4
                arrived(parts.at[j, other], part_recv.at[j, other])
                own[...] += parts[j, other]

        value = nt(value - own[...], lower[pl.ds(PLACE[j, j] * TILE, TILE), :], HIGHEST)
        value = jnp.where(pivot & (col < j), 0.0, value)
        solved.append(value)
        out_ref[:, j * TILE : (j + 1) * TILE] = value

    for j in range(4):
        solve(j, rest(j))

    @pl.when(row != 0)
    def _():
        arrived(feat_land.at[:, :, pl.ds(0, B // 2)], share_send)
        arrived(lower.at[pl.ds(0, 5 * TILE), :], share_send)
        arrived(pair, pair_send)
        arrived(parts.at[:, pl.ds(0, 3)], part_send)

    @pl.when(row == 0)
    def _():
        arrived(pair.at[:, pl.ds(0, 2)], pair_send)

        @pl.when(pivot)
        def _():
            arrived(parts.at[:, pl.ds(0, 2)], part_send)

        @pl.when(jnp.logical_not(pivot))
        def _():
            arrived(parts.at[:, 0], part_send)

    for t in range(4):
        for d in range(4):
            @pl.when(sends[t][d] == 1)
            def _():
                arrived(land.at[:, pl.ds(0, SUB), :], piece_send.at[t, d])
                arrived(feat_at(t, 0), feat_send.at[t, d])
                arrived(lower.at[pl.ds(0, 5 * SUB), :], low_send.at[t, d])

    @pl.when(row == 0)
    def _():
        for phase in range(2):
            arrived(gram_parts.at[pl.ds(0, 7)], gram_send.at[phase])


def on_device(features, factor):
    dma = pltpu.SemaphoreType.DMA
    return pl.pallas_call(
        body,
        out_shape=pltpu.VMEM((TILE, B), F32),
        in_specs=[pl.BlockSpec(memory_space=pl.ANY)] * 2,
        out_specs=pl.BlockSpec(memory_space=pltpu.VMEM),
        scratch_shapes=[
            pltpu.VMEM((2, ROWS, SLAB), F32),
            pltpu.VMEM((SLABS, ROWS, SLAB), BF16),
            pltpu.VMEM((SLABS, ROWS, SLAB), BF16),
            pltpu.VMEM((PIECES, TILE, SLAB), F32),
            pltpu.VMEM((4, 40, B), F32),
            pltpu.VMEM((4, ROWS, TILE), F32),
            pltpu.VMEM((4, 4, TILE, TILE), F32),
            pltpu.VMEM((4, 4, TILE, TILE), F32),
            pltpu.VMEM((TILE, TILE), F32),
            pltpu.VMEM((10 * TILE, TILE), F32),
            pltpu.VMEM((8, SHARE, TILE), F32),
            pltpu.VMEM((10 * TILE, TILE), F32),
            pltpu.VMEM((10 * TILE, TILE), F32),
            pltpu.VMEM((TILE, TILE), F32),
            pltpu.VMEM((TILE, B), F32),
            pltpu.VMEM((FEAT, TILE), F32),
            pltpu.VMEM((FEAT, B), F32),
            dma((2,)),
            dma((2, 2)),
            dma((4, 4)),
            dma((PIECES, 4)),
            dma((4, 4)),
            dma((4,)),
            dma((4, 4)),
            dma((4, 4)),
            dma,
            dma((4,)),
            dma,
            dma((4, 4)),
            dma((2,)),
            dma((2, 8)),
            dma,
            dma((5, 4)),
        ],
        compiler_params=pltpu.CompilerParams(
            collective_id=0, has_side_effects=True, vmem_limit_bytes=56 << 20
        ),
    )(features, factor)


def solution(mesh):
    placed = (P(None, "row"), P("row", "col"))
    return jax.shard_map(
        on_device, mesh=mesh, in_specs=placed, out_specs=P(("row", "col"), None), check_vma=False
    )
```

```python
import functools

import jax
import jax.numpy as jnp
from jax import lax
from jax.experimental import pallas as pl
from jax.experimental.pallas import tpu as pltpu
from jax.sharding import PartitionSpec as P

MESH = pl.DeviceIdType.MESH
HIGHEST = lax.Precision.HIGHEST
F32, BF16 = jnp.float32, jnp.bfloat16

B = 512
FEAT = 136
RIDGE = 40.0
TILE = 128
STRIP = 16
ROWS = 1024
SLAB = 512
SLABS = 8
PIECES = 32
SUB = 32
AHEAD = 8
ITEMS = PIECES + 1 + 4

TREES = (
    (1, 48, 64, 48, 27, 39, 53, 36, 41, 49, 65, 49, 48, 64, 80, 64),
    (2, 23, 35, 48, 48, 40, 50, 64, 64, 58, 66, 80, 48, 46, 50, 64),
    (4, 48, 64, 48, 48, 64, 80, 64, 38, 52, 68, 52, 30, 33, 53, 45),
    (8, 48, 44, 29, 48, 64, 56, 43, 64, 80, 72, 58, 48, 64, 56, 34),
)
BLOCKS = [(i, j) for j in range(4) for i in range(j, 4)]
PLACE = {b: n for n, b in enumerate(BLOCKS)}
COLUMN = [PLACE[j, j] * TILE for j in range(4)]
SHARE = len(BLOCKS) * TILE // 8


def lag(depth):
    return depth * 7 // 2 - 2


def pick(index, table):
    value = jnp.int32(0)
    for n, entry in enumerate(table):
        value = value + jnp.where(index == n, jnp.int32(entry), jnp.int32(0))
    return value


def nt(a, b, precision=None):
    return lax.dot_general(
        a, b, (((1,), (1,)), ((), ())), precision=precision, preferred_element_type=F32
    )


def tn(a, b, precision=None):
    return lax.dot_general(
        a, b, (((0,), (0,)), ((), ())), precision=precision, preferred_element_type=F32
    )


def two_parts(x):
    high = x.astype(BF16)
    return high, (x - high.astype(F32)).astype(BF16)


def three_parts(x):
    high = x.astype(BF16)
    rest = x - high.astype(F32)
    middle = rest.astype(BF16)
    return high, middle, (rest - middle.astype(F32)).astype(BF16)


def covariance(points, anchors):
    products = tn(points, anchors, HIGHEST)
    norm_points = tn(points * points, jnp.ones((FEAT, TILE), F32), HIGHEST)[:, :1]
    norm_anchors = jnp.sum(anchors * anchors, axis=0, keepdims=True)
    distance = norm_points + norm_anchors - 2.0 * products
    return products * (1.0 / FEAT) + jnp.exp(distance * (-0.5 / FEAT))


def invert_factor(t_ref):
    ri = lax.broadcasted_iota(jnp.int32, (STRIP, TILE), 0)
    ci = lax.broadcasted_iota(jnp.int32, (STRIP, TILE), 1)
    rj = lax.broadcasted_iota(jnp.int32, (TILE, TILE), 0)
    cj = lax.broadcasted_iota(jnp.int32, (TILE, TILE), 1)

    def strip(k, carry):
        first = pl.multiple_of(k * STRIP, STRIP)
        rows = t_ref[pl.ds(first, STRIP), :]
        turned = pltpu.roll(rows, TILE - first, 1)
        cols = [jnp.broadcast_to(turned[:, c : c + 1], (STRIP, TILE)) for c in range(STRIP)]
        rows = jnp.where((ci >= first) & (ci < first + STRIP), (ci - first == ri).astype(F32), rows)
        pivots = jnp.ones((STRIP, TILE), F32)
        for c in range(STRIP):
            pivot = jnp.broadcast_to(cols[c][c : c + 1, :], (STRIP, TILE))
            pivots = jnp.where(ri == c, pivot, pivots)
            factor = jnp.where(ri > c, cols[c] * (1.0 / pivot), 0.0)
            for d in range(c + 1, STRIP):
                cols[d] = cols[d] - factor * cols[d][c : c + 1, :]
            rows = rows - factor * rows[c : c + 1, :]
        scale = lax.rsqrt(pivots)
        scale = scale * (1.5 - 0.5 * pivots * scale * scale)
        rows = rows * scale
        lh, lm, ll = three_parts(jnp.where(ci >= first + STRIP, rows, 0.0))
        rh, rm, rl = three_parts(rows)
        change = tn(
            jnp.concatenate([lh, lh, lm, lh, lm, ll], 0),
            jnp.concatenate([rh, rm, rh, rl, rm, rh], 0),
        )
        below = (cj >= first) & (cj < first + STRIP) & (rj >= first + STRIP)
        t_ref[...] = jnp.where(below, 0.0, t_ref[...]) - change
        t_ref[pl.ds(first, STRIP), :] = jnp.where(ci < first + STRIP, rows, 0.0)
        return carry

    lax.fori_loop(0, TILE // STRIP, strip, 0)


def body(
    feat_ref, factor_ref, out_ref,
    stage, high, low, land, feat_land, sums, pair, parts, own, gram, gram_parts, gram_all, lower, tile, slab_kernel,
    points, pivots, points_sem, stage_sem, piece_send, piece_recv, feat_send, feat_recv, low_send, low_recv,
    pair_send, pair_recv, part_send, part_recv, gram_send, gram_recv, share_send, share_recv,
):
    row, col = lax.axis_index("row"), lax.axis_index("col")
    x, z = row // 4, row % 4
    near = [((x + 1) % 4) * 4 + z, x * 4 + (z + 1) % 4, ((x + 3) % 4) * 4 + z, x * 4 + (z + 3) % 4]
    codes = [pick(row, table) for table in TREES]
    depth = [code // 16 for code in codes]
    sends = [[(code // (1 << d)) % 2 for d in range(4)] for code in codes]
    peers = [(col + n) % 8 for n in range(1, 8)]
    y, core = col // 2, col % 2
    sibling = y * 2 + 1 - core
    pivot = (row == 0) & (col < 4)
    lags = [lag(d) for d in depth]
    last = jnp.maximum(jnp.maximum(lags[0], lags[1]), jnp.maximum(lags[2], lags[3]))

    barrier = pltpu.get_barrier_semaphore()
    for d in range(4):
        pl.semaphore_signal(barrier, inc=1, device_id=(near[d], col), device_id_type=MESH)
    for peer in peers:
        pl.semaphore_signal(barrier, inc=1, device_id=(row, peer), device_id_type=MESH)
    pl.semaphore_wait(barrier, 11)

    def remote(src, dst, send, recv, device):
        return pltpu.make_async_remote_copy(
            src_ref=src, dst_ref=dst, send_sem=send, recv_sem=recv, device_id=device, device_id_type=MESH
        )

    def arrived(ref, sem):
        pltpu.make_async_copy(ref, ref, sem).wait()

    def piece_at(n, t):
        return land.at[n, pl.ds(t * SUB, SUB), :]

    def low_at(j, t, c):
        size = SUB // 2 * (4 - j)
        return lower.at[pl.ds(pl.multiple_of(COLUMN[j] + (2 * t + c) * size, 16), size), :]

    def feat_at(t, c):
        return feat_land.at[t, :, pl.ds(pl.multiple_of(c * (B // 2), TILE), B // 2)]

    def exchange(ref, item, t):
        remote(ref, ref, share_send, share_recv.at[item, t], (row, sibling)).start()

    def send_piece(src, n, t, d):
        remote(src, piece_at(n, t), piece_send.at[t, d], piece_recv.at[n, t], (near[d], col)).start()

    def send_features(src, t, d):
        remote(src, feat_at(t, core), feat_send.at[t, d], feat_recv.at[t], (near[d], col)).start()

    def send_low(j, t, d):
        remote(low_at(j, t, core), low_at(j, t, core), low_send.at[t, d], low_recv.at[j, t], (near[d], col)).start()

    def accumulate(slab, block, panel, first=0, count=ROWS):
        panel_high, panel_low = panel
        at = pl.ds(first, count)
        a = nt(high[slab, at, :], jnp.concatenate([panel_high, panel_low], 0))
        b = nt(low[slab, at, :], panel_high)
        sums[block, at, :] += a[:, :TILE] + a[:, TILE:] + b

    def owned(q, c):
        return pl.ds(pl.multiple_of((q * 2 + c) * TILE, TILE), TILE)

    def send_pair(block, first, end=4):
        for q in range(first, end):
            src = sums.at[block, owned(q, 1 - core), :]
            remote(src, pair.at[block, q], pair_send, pair_recv.at[block], (row, sibling)).start()

    def send_parts(block, first):
        arrived(pair.at[block, pl.ds(first, 4 - first)], pair_recv.at[block])
        for q in range(first, 4):
            sums[block, owned(q, core), :] += pair[block, q]

            @pl.when(q != y)
            def _():
                src = sums.at[block, owned(q, core), :]
                remote(src, parts.at[block, y], part_send, part_recv.at[block, y], (row, q * 2 + core)).start()

    own_points = pltpu.make_async_copy(
        feat_ref.at[:, pl.ds(pl.multiple_of(col * TILE, TILE), TILE)], points, points_sem.at[0]
    )
    own_points.start()

    @pl.when(row == 0)
    def root():
        def start_piece(n, carry):
            block, slab = n // SLABS, n % SLABS
            for t in range(4):
                src = factor_ref.at[
                    pl.ds(pl.multiple_of(block * TILE + t * SUB, SUB), SUB),
                    pl.ds(pl.multiple_of(slab * SLAB, SLAB), SLAB),
                ]
                send_piece(src, n, t, t)
            return carry

        lax.fori_loop(0, AHEAD, start_piece, 0)
        sums[...] = jnp.zeros_like(sums)

        def load(half, slab):
            return pltpu.make_async_copy(
                factor_ref.at[pl.ds(half * 512, 512), pl.ds(pl.multiple_of(slab * SLAB, SLAB), SLAB)],
                stage.at[slab % 2, pl.ds(half * 512, 512), :],
                stage_sem.at[half, slab % 2],
            )

        def product(half, begin, end):
            def one(slab, carry):
                if half == 0:
                    carry = lax.fori_loop(AHEAD + slab * 3, AHEAD + slab * 3 + 3, start_piece, carry)
                load(half, slab).wait()
                h, l = two_parts(stage[slab % 2, pl.ds(half * 512, 512), :])
                high[slab, pl.ds(half * 512, 512), :] = h
                low[slab, pl.ds(half * 512, 512), :] = l

                @pl.when(slab + 2 < SLABS)
                def _():
                    load(half, slab + 2).start()

                panel_high, panel_low = high[slab, :512], low[slab, :512]
                if half == 0:
                    total = nt(h, panel_high * 0.5) + nt(h, panel_low)
                else:
                    total = nt(h, panel_high) + nt(h, panel_low) + nt(l, panel_high)
                for block in range(4):
                    sums[block, pl.ds(half * 512, 512), :] += total[:, block * TILE : (block + 1) * TILE]
                return carry

            lax.fori_loop(begin, end, one, 0)

        pivot_points = pltpu.make_async_copy(feat_ref.at[:, pl.ds(0, B)], pivots, points_sem.at[1])
        pivot_points.start()
        for half in range(2):
            load(half, 0).start()
            load(half, 1).start()
        product(0, 0, SLABS)
        for t in range(4):
            half = pl.ds(pl.multiple_of(core * (B // 2), TILE), B // 2)
            send_features(feat_ref.at[pl.ds(32 * t, 40), half], t, t)
        for n, (i, j) in enumerate(BLOCKS):
            gram[pl.ds(n * TILE, TILE), :] = sums[j, pl.ds(i * TILE, TILE), :] + sums[i, pl.ds(j * TILE, TILE), :].T
        mine = pl.ds(pl.multiple_of(col * SHARE, SHARE), SHARE)
        for peer in peers:
            src = gram.at[pl.ds(pl.multiple_of(peer * SHARE, SHARE), SHARE), :]
            remote(src, gram_parts.at[col], gram_send.at[0], gram_recv.at[0, col], (row, peer)).start()
        product(1, 0, 4)
        share = gram[mine, :]
        for peer in peers:
            arrived(gram_parts.at[peer], gram_recv.at[0, peer])
            share = share + gram_parts[peer]
        gram_all[mine, :] = share
        for peer in peers:
            remote(
                gram_all.at[mine, :], gram_all.at[mine, :], gram_send.at[1], gram_recv.at[1, col], (row, peer)
            ).start()
        pivot_points.wait()
        for j in range(4):
            size = (4 - j) * TILE
            values = covariance(pivots[:, j * TILE : B], pivots[:, j * TILE : (j + 1) * TILE])
            same = lax.broadcasted_iota(jnp.int32, (size, TILE), 0) == lax.broadcasted_iota(jnp.int32, (size, TILE), 1)
            lower[pl.ds(COLUMN[j], size), :] = values + jnp.where(same, RIDGE, 0.0)
        for peer in peers:
            arrived(gram_all.at[pl.ds(pl.multiple_of(peer * SHARE, SHARE), SHARE), :], gram_recv.at[1, peer])
        lower[...] = lower[...] - gram_all[...]

        def at(i, j):
            return pl.ds(PLACE[i, j] * TILE, TILE)

        for j in range(4):
            tile[...] = lower[at(j, j), :]
            invert_factor(tile)
            inverse = tile[...]
            lower[at(j, j), :] = inverse
            for i in range(j + 1, 4):
                lower[at(i, j), :] = nt(lower[at(i, j), :], inverse, HIGHEST)
            for t in range(4):
                send_low(j, t, t)
            for k in range(j + 1, 4):
                for i in range(k, 4):
                    lower[at(i, k), :] = lower[at(i, k), :] - nt(lower[at(i, j), :], lower[at(k, j), :], HIGHEST)
        product(1, 4, SLABS)
        for block in range(4):
            send_pair(block, 2)
        own_points.wait()
        slab_kernel[...] = covariance(points[...], pivots[...])
        for block in range(4):
            send_parts(block, 2)

    @pl.when(row != 0)
    def others():
        def load(slab):
            return pltpu.make_async_copy(
                factor_ref.at[:, pl.ds(pl.multiple_of(slab * SLAB, SLAB), SLAB)],
                stage.at[slab % 2],
                stage_sem.at[0, slab % 2],
            )

        load(0).start()
        load(1).start()
        sums[...] = jnp.zeros_like(sums)

        def slot(s, carry):
            @pl.when(s - last == PIECES)
            def _():
                send_parts(3, 0)

            for t in range(4):
                item = s - lags[t]

                @pl.when((item >= 0) & (item < PIECES))
                def _():
                    arrived(piece_at(item, t), piece_recv.at[item, t])
                    for d in range(4):
                        @pl.when(sends[t][d] == 1)
                        def _():
                            send_piece(piece_at(item, t), item, t, d)

                @pl.when((item >= PIECES) & (item < ITEMS))
                def _():
                    @pl.when(item == PIECES)
                    def _():
                        arrived(feat_at(t, core), feat_recv.at[t])
                        for d in range(4):
                            @pl.when(sends[t][d] == 1)
                            def _():
                                send_features(feat_at(t, core), t, d)
                        exchange(feat_at(t, core), 4, t)

                    for j in range(4):
                        @pl.when(item == PIECES + 1 + j)
                        def _():
                            arrived(low_at(j, t, core), low_recv.at[j, t])
                            for d in range(4):
                                @pl.when(sends[t][d] == 1)
                                def _():
                                    send_low(j, t, d)
                            exchange(low_at(j, t, core), j, t)

            @pl.when(s < SLABS)
            def _():
                load(s).wait()
                h, l = two_parts(stage[s % 2])
                high[s] = h
                low[s] = l

                @pl.when(s + 2 < SLABS)
                def _():
                    load(s + 2).start()

            m = s - last

            @pl.when(m == PIECES + 2)
            def _():
                for t in range(4):
                    arrived(feat_at(t, 1 - core), share_recv.at[4, t])
                anchors = jnp.concatenate([feat_land[t, :32] for t in range(3)] + [feat_land[3]], 0)
                own_points.wait()
                slab_kernel[...] = covariance(points[...], anchors)

            @pl.when(m == PIECES - 1)
            def _():
                panel = two_parts(land[PIECES - 1])
                for q in (0, 2):
                    accumulate(SLABS - 1, 3, panel, q * 2 * TILE, ROWS // 2)
                    send_pair(3, q, q + 2)

            @pl.when((m >= 0) & (m < PIECES - 1))
            def _():
                block, slab = m // SLABS, m % SLABS
                accumulate(slab, block, two_parts(land[m]))

                @pl.when(slab == SLABS - 1)
                def _():
                    send_pair(block, 0)

                @pl.when((slab == 1) & (block > 0))
                def _():
                    send_parts(block - 1, 0)

            return carry

        lax.fori_loop(0, ITEMS + last, slot, 0)

    solved = []
    rows = lax.broadcasted_iota(jnp.int32, (TILE, TILE), 0) + row * ROWS + col * TILE
    columns = lax.broadcasted_iota(jnp.int32, (TILE, TILE), 1)

    def rest(j):
        @pl.when(row != 0)
        def _():
            for t in range(4):
                arrived(low_at(j, t, 1 - core), share_recv.at[j, t])

        value = slab_kernel[:, j * TILE : (j + 1) * TILE]
        value = value + jnp.where(rows == columns + j * TILE, RIDGE, 0.0)
        for i in range(j):
            value = value - nt(solved[i], lower[pl.ds(PLACE[j, i] * TILE, TILE), :], HIGHEST)
        return value

    def solve(j, value):
        @pl.when(pivot)
        def _():
            place = COLUMN[j] + jnp.maximum(col - j, 0) * TILE
            own[...] = gram_all[pl.ds(pl.multiple_of(place, TILE), TILE), :]

        @pl.when(jnp.logical_not(pivot))
        def _():
            own[...] = sums[j, owned(y, core), :]
            for n in range(1, 4):
                other = (y + n) % 4
                arrived(parts.at[j, other], part_recv.at[j, other])
                own[...] += parts[j, other]

        value = nt(value - own[...], lower[pl.ds(PLACE[j, j] * TILE, TILE), :], HIGHEST)
        value = jnp.where(pivot & (col < j), 0.0, value)
        solved.append(value)
        out_ref[:, j * TILE : (j + 1) * TILE] = value

    for j in range(3):
        solve(j, rest(j))
    remainder = rest(3)

    @pl.when(row != 0)
    def _():
        arrived(feat_land.at[:, :, pl.ds(0, B // 2)], share_send)
        arrived(lower.at[pl.ds(0, 5 * TILE), :], share_send)
        arrived(pair, pair_send)

    @pl.when(row == 0)
    def _():
        arrived(pair.at[:, pl.ds(0, 2)], pair_send)

    for t in range(4):
        for d in range(4):
            @pl.when(sends[t][d] == 1)
            def _():
                arrived(land.at[:, pl.ds(0, SUB), :], piece_send.at[t, d])
                arrived(feat_at(t, 0), feat_send.at[t, d])
                arrived(lower.at[pl.ds(0, 5 * SUB), :], low_send.at[t, d])

    @pl.when(row == 0)
    def _():
        for phase in range(2):
            arrived(gram_parts.at[pl.ds(0, 7)], gram_send.at[phase])

    solve(3, remainder)

    @pl.when(row != 0)
    def _():
        arrived(parts.at[:, pl.ds(0, 3)], part_send)

    @pl.when(row == 0)
    def _():
        @pl.when(pivot)
        def _():
            arrived(parts.at[:, pl.ds(0, 2)], part_send)

        @pl.when(jnp.logical_not(pivot))
        def _():
            arrived(parts.at[:, 0], part_send)


def on_device(features, factor):
    dma = pltpu.SemaphoreType.DMA
    return pl.pallas_call(
        body,
        out_shape=pltpu.VMEM((TILE, B), F32),
        in_specs=[pl.BlockSpec(memory_space=pl.ANY)] * 2,
        out_specs=pl.BlockSpec(memory_space=pltpu.VMEM),
        scratch_shapes=[
            pltpu.VMEM((2, ROWS, SLAB), F32),
            pltpu.VMEM((SLABS, ROWS, SLAB), BF16),
            pltpu.VMEM((SLABS, ROWS, SLAB), BF16),
            pltpu.VMEM((PIECES, TILE, SLAB), F32),
            pltpu.VMEM((4, 40, B), F32),
            pltpu.VMEM((4, ROWS, TILE), F32),
            pltpu.VMEM((4, 4, TILE, TILE), F32),
            pltpu.VMEM((4, 4, TILE, TILE), F32),
            pltpu.VMEM((TILE, TILE), F32),
            pltpu.VMEM((10 * TILE, TILE), F32),
            pltpu.VMEM((8, SHARE, TILE), F32),
            pltpu.VMEM((10 * TILE, TILE), F32),
            pltpu.VMEM((10 * TILE, TILE), F32),
            pltpu.VMEM((TILE, TILE), F32),
            pltpu.VMEM((TILE, B), F32),
            pltpu.VMEM((FEAT, TILE), F32),
            pltpu.VMEM((FEAT, B), F32),
            dma((2,)),
            dma((2, 2)),
            dma((4, 4)),
            dma((PIECES, 4)),
            dma((4, 4)),
            dma((4,)),
            dma((4, 4)),
            dma((4, 4)),
            dma,
            dma((4,)),
            dma,
            dma((4, 4)),
            dma((2,)),
            dma((2, 8)),
            dma,
            dma((5, 4)),
        ],
        compiler_params=pltpu.CompilerParams(
            collective_id=0, has_side_effects=True, vmem_limit_bytes=56 << 20
        ),
    )(features, factor)


def solution(mesh):
    placed = (P(None, "row"), P("row", "col"))
    return jax.shard_map(
        on_device, mesh=mesh, in_specs=placed, out_specs=P(("row", "col"), None), check_vma=False
    )
```
